32 devices in a mesh: trial: 2 (over x), freq: 4 (over y, core), lst: 4 (over z).
Axes of the slice: x: 2, y: 2, z: 4, core: 2. Of those that a mesh axis runs over, the one named last changes fastest.
Arguments:
- sky_east: bfloat16 [8192], P(('trial', 'freq')), parts along dimension 0, may hold values from -0.59765625 to 0.59765625
- sky_north: bfloat16 [8192], P(('trial', 'freq')), parts along dimension 0, may hold values from -0.59765625 to 0.59765625
- sky_flux: bfloat16 [8192], P(('trial', 'freq')), parts along dimension 0, may hold values from 0.19921875 to 5
- sky_scint: bfloat16 [8192, 1024], P(('trial', 'freq'), 'lst'), parts along dimension 0, may hold values from 0.19921875 to 1.796875
- visible: int32 [256, 32], P(('trial', 'lst')), parts along dimension 0, may hold values 0 or 1
- antenna_coords: float32 [350, 2], replicated, may hold values from -150 to 150, as said below
- baseline_antennas: int32 [256, 2], replicated, may hold values from 0 to 349, as said below
- filter_taps: bfloat16 [8, 257], P('freq'), may hold values from -0.375 to 0.375
Outputs:
- visibility: bfloat16 [16, 2, 256, 1024], P(('trial', 'freq'), None, None, 'lst'), parts along dimension 0
- filtered: bfloat16 [16, 2, 256, 1024], P(('trial', 'freq'), None, None, 'lst'), parts along dimension 0
The draws below stay inside these ranges and needn't reach their ends.
There are 2 independent parts, one for each index of `trial`. The reference program is written for one: setup_inputs(seed, part) draws one part's arguments, and reference() takes and returns one part's arrays. A program takes and returns all parts, laid end to end along the dimension named above; an argument that names none is the same for every part. Nothing has to cross between parts.
Inputs may be any that keep to these rules, and one draw needn't show every extreme that they name: `baseline_antennas`: each row names two different antennas. `antenna_coords`: positions in metres; no two antennas are closer than 11 metres.
All inputs are finite; a program needn't handle non-finite values. No bound on the sum of `visible` on one device may be relied on, other than what follows from the above.
Results may differ from the reference program's by a relative error of at most 0.0061.
Values may be sent and summed in bfloat16 or wider, within the bound.
A program may use at most 64 MiB of HBM per device.

```python
import math
import jax
import jax.numpy as jnp
from jax import lax

ANTENNA_COUNT = 350
BASELINE_COUNT = 256
SRC_BLOCK = 128
TAIL = 256
BLOCK_T = 8
TAPS = 257
SOURCES = 4096
CHANNELS = 8
TIME_SAMPLES = 1024
TIME_BLOCKS = 128
SRC_BLOCKS = 32


def draw_antenna_coords(key, part):
    grid_side = int(math.ceil(math.sqrt(ANTENNA_COUNT)))
    index_all = jnp.arange(ANTENNA_COUNT)
    grid_east = (index_all % grid_side).astype(jnp.float32)
    grid_north = (index_all // grid_side).astype(jnp.float32)
    centre_off = 0.5 * (grid_side - 1)
    jitter = jax.random.uniform(jax.random.fold_in(key, 11), (ANTENNA_COUNT, 2), jnp.float32, -2.0, 2.0)
    placed = jnp.stack([15.0 * (grid_east - centre_off), 15.0 * (grid_north - centre_off)], axis=1)
    return (placed + jitter).astype(jnp.float32)


def draw_baseline_antennas(key, part):
    leading_key = jax.random.fold_in(key, 21)
    trailing_key = jax.random.fold_in(key, 22)
    first_antenna = jax.random.randint(leading_key, (BASELINE_COUNT,), 0, ANTENNA_COUNT)
    lag_offsets = jax.random.randint(trailing_key, (BASELINE_COUNT,), 1, ANTENNA_COUNT)
    second_antenna = (first_antenna + lag_offsets) % ANTENNA_COUNT
    return jnp.stack([first_antenna, second_antenna], axis=1).astype(jnp.int32)


def plant(result, own_key, low, top_value):
    longest = result.shape.index(max(result.shape))
    spots = []
    for shift in (0, 1):
        where = [jax.random.randint(jax.random.fold_in(own_key, axis), (), 0, length) for axis, length in enumerate(result.shape)]
        where[longest] = (where[longest] + shift) % result.shape[longest]
        spots.append(tuple(where))
    return result.at[spots[0]].set(low).at[spots[1]].set(top_value)


def block_levels(rng, shape, cuts, least, largest):
    def one(position, blocks):
        draws = jax.random.uniform(jax.random.fold_in(jax.random.fold_in(rng, 6), position), (blocks,), jnp.float32, least / len(cuts), largest / len(cuts))
        return jnp.repeat(jnp.exp(draws), shape[position] // blocks).reshape((-1,) + (1,) * (len(shape) - position - 1))

    gain = one(*cuts[0])
    for cut in cuts[1:]:
        gain = gain * one(*cut)
    return gain


def scatter_about(stream_key, dims, scale, most, shards=(), held_as=jnp.bfloat16):
    result = jax.random.normal(stream_key, dims, jnp.float32) * scale
    if len(shards) > 0:
        result = block_levels(stream_key, dims, shards, -0.22, 0.18) * result
    return jnp.clip(result, min=-most, max=most).astype(held_as)


def setup_inputs(seed: int = 0, part: int = 0) -> dict:
    keys = jax.random.split(jax.random.key(seed), 9)
    own_keys = jax.random.split(jax.random.fold_in(keys[8], part), 9)
    return {
        "sky_east": jnp.clip(jax.random.uniform(own_keys[0], (SOURCES,), jnp.float32, -0.59765625, 0.59765625) * block_levels(own_keys[0], (SOURCES,), ((0, 4),), -0.4, 0.0), -0.59765625, 0.59765625).astype(jnp.bfloat16),
        "sky_north": jnp.clip(jax.random.uniform(own_keys[1], (SOURCES,), jnp.float32, -0.59765625, 0.59765625) * block_levels(own_keys[1], (SOURCES,), ((0, 4),), -0.4, 0.0), -0.59765625, 0.59765625).astype(jnp.bfloat16),
        "sky_flux": jnp.clip(jnp.exp(math.log(5.0) - 3.2227897 * jax.random.uniform(own_keys[2], (SOURCES,), jnp.float32) ** block_levels(own_keys[2], (SOURCES,), ((0, 4),), -0.2, 0.2)), 0.19921875, 5.0).astype(jnp.bfloat16),
        "sky_scint": jnp.clip(0.19921875 + 1.5976562 * jax.random.uniform(own_keys[3], (SOURCES, TIME_SAMPLES), jnp.float32) ** block_levels(own_keys[3], (SOURCES, TIME_SAMPLES), ((0, 4), (1, 4)), -0.2, 0.2), 0.19921875, 1.796875).astype(jnp.bfloat16),
        "visible": plant((jax.random.randint(own_keys[4], (TIME_BLOCKS, SRC_BLOCKS), 0, 4) < 3).astype(jnp.int32), jax.random.fold_in(own_keys[4], 1), 0, 1),
        "antenna_coords": draw_antenna_coords(jax.random.fold_in(keys[8], 71), part),
        "baseline_antennas": draw_baseline_antennas(jax.random.fold_in(keys[8], 71), part),
        "filter_taps": scatter_about(keys[7], (CHANNELS, TAPS), TAPS ** -0.5, 0.375, ((0, 4),)),
    }


C_LIGHT = 299792458.0
NU_START = 150000000.0
NU_STEP = 97656.25
OMEGA_STEP = 4.37526e-05
BEAM_SIGMA = 0.35
CENTRE_START = -0.045
TWO_PI = 2.0 * math.pi

def reference(sky_east, sky_north, sky_flux, sky_scint, visible, antenna_coords, baseline_antennas, filter_taps):
    sky_east = sky_east.astype(jnp.float32)
    sky_north = sky_north.astype(jnp.float32)
    sky_flux = sky_flux.astype(jnp.float32)
    first_antenna = baseline_antennas[:, 0].astype(jnp.int32)
    second_antenna = baseline_antennas[:, 1].astype(jnp.int32)
    baseline_east = antenna_coords[first_antenna, 0] - antenna_coords[second_antenna, 0]
    baseline_north = antenna_coords[first_antenna, 1] - antenna_coords[second_antenna, 1]
    chan_index = jnp.arange(CHANNELS).astype(jnp.int32).astype(jnp.float32)
    frequency = NU_START + NU_STEP * chan_index
    wavenum = TWO_PI * frequency / C_LIGHT
    beam_width = BEAM_SIGMA * NU_START / frequency
    samples = jnp.arange(TIME_SAMPLES).astype(jnp.int32).astype(jnp.float32)
    centre = CENTRE_START + OMEGA_STEP * samples
    seen_mask = jnp.repeat(jnp.repeat(visible.astype(jnp.float32).T, SRC_BLOCK, axis=0), BLOCK_T, axis=1)
    seen_mask = seen_mask * sky_scint.astype(jnp.float32)
    geometry = baseline_east[:, None] * sky_east[None, :] + baseline_north[:, None] * sky_north[None, :]
    scale_norm = 1.0 / math.sqrt(SOURCES)

    def channel(inputs):
        wave, width = inputs
        phases = wave * geometry
        planes = jnp.concatenate([jnp.cos(phases), -jnp.sin(phases)], axis=0).astype(jnp.bfloat16)
        beam_gain = jnp.exp(-((sky_east[:, None] - centre[None, :]) ** 2 + (sky_north ** 2)[:, None]) / (2.0 * width * width))
        amplitude = ((sky_flux * scale_norm)[:, None] * beam_gain * seen_mask).astype(jnp.bfloat16)
        summed_terms = jnp.dot(planes, amplitude, preferred_element_type=jnp.float32)
        real_component = summed_terms[:BASELINE_COUNT]
        imaginary_component = summed_terms[BASELINE_COUNT:]
        fringe = (wave * baseline_east)[:, None] * (OMEGA_STEP * samples)[None, :]
        vis_real = jnp.cos(fringe) * real_component + jnp.sin(fringe) * imaginary_component
        vis_imag = jnp.cos(fringe) * imaginary_component - jnp.sin(fringe) * real_component
        return jnp.stack([vis_real, vis_imag], axis=0).astype(jnp.bfloat16)
    visibility = lax.map(channel, (wavenum, beam_width))

    def smooth(inputs):
        visibility_channel, taps_chan = inputs
        lag_index = jnp.arange(TIME_SAMPLES).astype(jnp.int32)[None, :] - jnp.arange(TIME_SAMPLES).astype(jnp.int32)[:, None]
        inside = (lag_index >= 0) & (lag_index <= TAIL)
        toeplitz = jnp.where(inside, taps_chan[jnp.clip(lag_index, 0, TAIL)], 0.0).astype(jnp.bfloat16)
        every_row = visibility_channel.reshape(2 * BASELINE_COUNT, TIME_SAMPLES)
        filtered_output = jnp.dot(every_row, toeplitz, preferred_element_type=jnp.float32)
        return filtered_output.astype(jnp.bfloat16).reshape(2, BASELINE_COUNT, TIME_SAMPLES)
    filtered = lax.map(smooth, (visibility, filter_taps))
    return (visibility, filtered)
```

```python
import functools
import math

import jax
import jax.numpy as jnp
import numpy as np
from jax import lax
from jax.experimental import pallas as pl
from jax.experimental.pallas import tpu as pltpu
from jax.sharding import PartitionSpec as P

SRC_BLOCK = 128
TAIL = 256
BLOCK_T = 8

C_LIGHT = 299792458.0
NU_START = 150000000.0
NU_STEP = 97656.25
OMEGA_STEP = 4.37526e-05
BEAM_SIGMA = 0.35
CENTRE_START = -0.045
LOG2E = math.log2(math.e)
ROUNDER = 1.5 * 2.0**23
ROWS = 16
GROUPS = 4
TILE = 256
AMP_TILE = 32
AMP_STEP = 256
MESH = pl.DeviceIdType.MESH
F32 = jnp.float32
BF16 = jnp.bfloat16


def fit_even(fun, reach, degree):
    nodes = np.cos((np.arange(400) + 0.5) * np.pi / 400)
    z = 0.5 * reach * reach * (nodes + 1.0)
    cheb = np.polynomial.chebyshev.Chebyshev.fit(z, fun(np.sqrt(z)), degree, domain=[0.0, reach * reach])
    return [float(c) for c in cheb.convert(kind=np.polynomial.Polynomial).coef]


def cos_turn(x):
    return np.cos(2.0 * np.pi * x)


def sin_turn(x):
    return np.sin(2.0 * np.pi * x) / x


COS_FULL = fit_even(cos_turn, 0.5, 5)
SIN_FULL = fit_even(sin_turn, 0.5, 4)
STEP_REACH = 0.12
COS_STEP = fit_even(cos_turn, STEP_REACH, 3)
SIN_STEP = fit_even(sin_turn, STEP_REACH, 2)


def horner(coefs, z):
    total = coefs[-1] * z + coefs[-2]
    for c in coefs[-3::-1]:
        total = total * z + c
    return total


def cos_minus_sin(turns):
    r = turns - ((turns + ROUNDER) - ROUNDER)
    z = r * r
    return horner(COS_FULL, z), horner([-c for c in SIN_FULL], z) * r


def sincos_turns(turns):
    r = turns - ((turns + ROUNDER) - ROUNDER)
    z = r * r
    return horner(COS_FULL, z), horner(SIN_FULL, z) * r


def sincos_step(r):
    z = r * r
    return horner(COS_STEP, z), horner(SIN_STEP, z) * r


def pieces(x):
    high = x.astype(BF16).astype(F32)
    middle = (x - high).astype(BF16).astype(F32)
    low = (x - high - middle).astype(BF16).astype(F32)
    return high, middle, low


def rowdot(a, b):
    return lax.dot_general(a, b, (((0,), (0,)), ((), ())), preferred_element_type=F32)


def kernel(
    dims,
    east_ref, north_ref, flux_ref, visible_ref, coords_ref, pairs_ref, taps_ref, scint_hbm,
    vis_hbm, out_hbm,
    scint, vis, out, phase_rows, beam_cols, beam_right, planes, amps, mask_rows, coefs, lines, toep, tap_rows, tail,
    totals, pair_out, pair_in, far_out, far_in,
    scint_sem, pair_send, pair_recv, far_send, far_recv, halo_send, halo_recv, vis_sem, out_sem,
):
    n_freq, n_lst, chans = dims
    local_src, times = scint.shape
    count = pairs_ref.shape[1]
    group = count // GROUPS
    chips = n_freq // 2
    per_chip = 2 * chans
    n_chan = chips * per_chip
    total_src = local_src * n_freq
    blocks = local_src // SRC_BLOCK
    me = lax.axis_index("freq")
    lst = lax.axis_index("lst")
    chip, core = me // 2, me % 2
    partner = chip * 2 + (1 - core)

    scint_copy = pltpu.make_async_copy(scint_hbm, scint, scint_sem)
    scint_copy.start()

    barrier = pltpu.get_barrier_semaphore()
    pl.semaphore_signal(barrier, inc=1, device_id={"freq": partner}, device_id_type=MESH)
    for d in range(1, chips):
        pl.semaphore_signal(
            barrier, inc=1, device_id={"freq": ((chip + d) % chips) * 2 + core}, device_id_type=MESH
        )

    @pl.when(lst > 0)
    def _():
        pl.semaphore_signal(barrier, inc=1, device_id={"lst": lst - 1}, device_id_type=MESH)

    def send(src, dst, ssem, rsem, to):
        return pltpu.make_async_remote_copy(
            src_ref=src, dst_ref=dst, send_sem=ssem, recv_sem=rsem, device_id=to, device_id_type=MESH
        )

    rising = chip * 2 >= chips
    way = jnp.where(rising, 1, -1)
    way_f = way.astype(F32)
    first = jnp.where(rising, 0, n_chan - 1).astype(F32)
    nu_first = NU_START + NU_STEP * first
    own_place = jnp.where(rising, chip, chips - 1 - chip)
    own_half = jnp.where(rising, core, 1 - core)
    nus = [NU_START + NU_STEP * (me * chans + c).astype(F32) for c in range(chans)]

    def place_of(d):
        return (own_place + d) % chips

    def chip_at(d):
        place = place_of(d)
        return jnp.where(rising, place, chips - 1 - place)

    def channel_at(q):
        return jnp.where(rising, q, chans - 1 - q)

    antennas = coords_ref.shape[1]
    ids = lax.broadcasted_iota(jnp.int32, (antennas, count), 0)
    select = (pairs_ref[0:1, :] == ids).astype(F32) - (pairs_ref[1:2, :] == ids).astype(F32)
    both = jnp.dot(coords_ref[...], select, precision=lax.Precision.HIGHEST, preferred_element_type=F32)
    east = jnp.broadcast_to(both[0:1, :], (128, count)).T
    north = jnp.broadcast_to(both[1:2, :], (128, count)).T
    lane = lax.broadcasted_iota(jnp.int32, (count, 128), 1)
    pair_value = jnp.where(lane < 3, east, jnp.where(lane < 6, north, 0.0))

    def coef_rows(scale):
        high, middle, low = pieces(pair_value * scale)
        picked = jnp.where((lane == 0) | (lane == 3), high, jnp.where((lane == 1) | (lane == 4), middle, low))
        return picked.astype(BF16)[:, :ROWS]

    main = coef_rows(nu_first * (1.0 / C_LIGHT))
    step = coef_rows(way_f * (NU_STEP / C_LIGHT))
    for g in range(GROUPS):
        coefs[g, 0:group, :] = main[g * group : (g + 1) * group]
        coefs[g, group : 2 * group, :] = step[g * group : (g + 1) * group]
    lines[...] = east

    t_blocks = visible_ref.shape[0]
    spread = (
        lax.broadcasted_iota(jnp.int32, (t_blocks, times), 1) // BLOCK_T
        == lax.broadcasted_iota(jnp.int32, (t_blocks, times), 0)
    ).astype(BF16)
    mask_rows[...] = rowdot(visible_ref[...].astype(F32).astype(BF16), spread)

    samples = (lst * times + lax.broadcasted_iota(jnp.int32, (1, times), 1)).astype(F32)
    centre = CENTRE_START + OMEGA_STEP * samples
    row_id = lax.broadcasted_iota(jnp.int32, (ROWS, times), 0)
    delta = NU_STEP / NU_START
    broad = 0.5 * LOG2E / (BEAM_SIGMA * BEAM_SIGMA)
    ratio = nu_first * (1.0 / NU_START)
    half = broad * ratio * ratio
    slope = broad * delta * way_f * (2.0 * ratio + delta * way_f)
    bend = 2.0 * broad * delta * delta / slope
    for at, scale, offset in ((0, half, 3), (1, slope, 9)):
        table = jnp.where((row_id >= offset) & (row_id < offset + 3), 1.0, 0.0)
        for base, rows in ((0, pieces(centre * (2.0 * scale))), (6, pieces(centre * centre * (-scale)))):
            for i, row in enumerate(rows):
                table = jnp.where(row_id == base + i, row, table)
        beam_right[:, at * times : (at + 1) * times] = table.astype(BF16)

    l_all = east_ref[...].astype(F32)
    m_all = north_ref[...].astype(F32)
    radius = l_all * l_all + m_all * m_all
    level = jnp.log(flux_ref[...].astype(F32) * (1.0 / math.sqrt(total_src))) * LOG2E - radius * half
    level_rows = pieces(level)
    slope_rows = pieces(radius * (-slope))
    src_row = lax.broadcasted_iota(jnp.int32, (ROWS, SRC_BLOCK), 0)
    for k in range(blocks):
        at = slice(k, k + 1)
        rows = slice(k * SRC_BLOCK, (k + 1) * SRC_BLOCK)
        l = l_all[at]
        phase_rows[:, rows] = jnp.where(src_row < 3, l, jnp.where(src_row < 6, m_all[at], 0.0)).astype(BF16)
        table = jnp.where(src_row < 3, l, jnp.where(src_row < 9, 1.0, 0.0))
        for base, values in ((3, level_rows), (9, slope_rows)):
            for i, value in enumerate(values):
                table = jnp.where(src_row == base + i, value[at], table)
        beam_cols[rows, :] = table.T.astype(BF16)

    scint_copy.wait()

    @pl.loop(0, local_src // AMP_STEP)
    def _(i):
        for k in range(AMP_STEP // AMP_TILE):
            rows = pl.ds(pl.multiple_of(i * AMP_STEP + k * AMP_TILE, AMP_TILE), AMP_TILE)
            power = jnp.dot(beam_cols[rows, :], beam_right[...], preferred_element_type=F32)
            block = i * (AMP_STEP // SRC_BLOCK) + k // (SRC_BLOCK // AMP_TILE)
            mask = mask_rows[pl.ds(me * blocks + block, 1), :]
            value = jnp.exp2(power[:, :times]) * (scint[rows, :].astype(F32) * mask)
            gain = jnp.exp2(power[:, times:])
            change = jnp.exp2(power[:, times:] * bend)
            for p in range(n_chan):
                amps[p, rows, :] = value.astype(BF16)
                if p < n_chan - 1:
                    value = value * gain
                if p < n_chan - 2:
                    gain = gain * change

    def trig(g):
        @pl.loop(0, local_src // TILE)
        def _(i):
            cols = pl.ds(pl.multiple_of(i * TILE, TILE), TILE)
            turns = jnp.dot(coefs[g], phase_rows[:, cols], preferred_element_type=F32)
            co, si = cos_minus_sin(turns[:group])
            cd, sd = sincos_step(turns[group:])
            twice = cd + cd
            older = None
            for p in range(n_chan):
                planes[p, 0:group, cols] = co.astype(BF16)
                planes[p, group : 2 * group, cols] = si.astype(BF16)
                if p == 0:
                    older, (co, si) = (co, si), (co * cd + si * sd, si * cd - co * sd)
                else:
                    older, (co, si) = (co, si), (twice * co - older[0], twice * si - older[1])

    def partial_sum(d, half, q):
        p = place_of(d) * per_chip + half * chans + q
        return jnp.dot(planes[p], amps[p], preferred_element_type=F32)

    def pair_copy(g, d):
        return send(pair_out.at[g, d], pair_in.at[g, d], pair_send.at[g, d], pair_recv.at[g, d], {"freq": partner})

    def far_copy(g, d, c):
        return send(
            far_out.at[g, d - 1, c], far_in.at[g, chip, c], far_send.at[g, d - 1, c], far_recv.at[g, chip, c],
            {"freq": chip_at(d) * 2 + core},
        )

    def far_arrival(g, d, c):
        src = (chip + d) % chips
        return send(
            far_in.at[g, src, c], far_in.at[g, src, c], far_send.at[g, d - 1, c], far_recv.at[g, src, c],
            {"freq": src * 2 + core},
        )

    def group_rows(g):
        return pl.ds(g * group if isinstance(g, int) else pl.multiple_of(g * group, group), group)

    def halo_copy(g, c):
        rows = group_rows(g)
        return send(
            vis.at[c, :, rows, :], tail.at[c, :, rows, :], halo_send.at[g, c], halo_recv.at[g, c], {"lst": (lst + 1) % n_lst}
        )

    def vis_copy(g, c):
        rows = group_rows(g)
        return pltpu.make_async_copy(vis.at[c, :, rows, :], vis_hbm.at[c, :, rows, :], vis_sem.at[g, c])

    def out_copy(g, c):
        rows = group_rows(g)
        return pltpu.make_async_copy(out.at[c, :, rows, :], out_hbm.at[c, :, rows, :], out_sem.at[g, c])

    pl.semaphore_wait(barrier, chips + (lst < n_lst - 1).astype(jnp.int32))

    @pl.when(lst == 0)
    def _():
        tail[...] = jnp.zeros_like(tail)

    def multiply(g, d):
        for q in range(chans):
            pair_out[g, d, q] = partial_sum(d, 1 - own_half, q).astype(BF16)
        for q in range(chans):
            totals[g, d, q] = partial_sum(d, own_half, q)
        pair_copy(g, d).start()

    def forward(g):
        for d in range(1, chips):
            pair_copy(g, d).wait_recv()
            for q in range(chans):
                c = channel_at(q)
                far_out[g, d - 1, c] = (totals[g, d, q] + pair_in[g, d, q].astype(F32)).astype(BF16)
                far_copy(g, d, c).start()

    def spread_taps():
        tap_rows[...] = jnp.zeros_like(tap_rows)
        tap_rows[0:chans, 0 : TAIL + 1] = taps_ref[...].astype(F32)
        for c in range(chans):
            wide = jnp.broadcast_to(tap_rows[c : c + 1, :], (TAIL + times, TAIL + times))
            skewed = pltpu.roll(wide, 0, 1, stride=1, stride_axis=0)
            toep[c] = skewed[:, TAIL:].astype(BF16)

    def finish(g):
        rows = group_rows(g)
        pair_copy(g, 0).wait_recv()
        for q in range(chans):
            c = channel_at(q)
            summed = totals[g, 0, q] + pair_in[g, 0, q].astype(F32)
            for d in range(1, chips):
                far_arrival(g, d, c).wait_recv()
                summed = summed + far_in[g, (chip + d) % chips, c].astype(F32)
            real, imag = summed[:group], summed[group:]
            scale = (NU_START + NU_STEP * (me * chans + c).astype(F32)) * (OMEGA_STEP / C_LIGHT)
            co, si = sincos_turns((lines[rows, 0:1] * scale) * samples)
            vis[c, 0, rows, :] = (co * real + si * imag).astype(BF16)
            vis[c, 1, rows, :] = (co * imag - si * real).astype(BF16)

            @pl.when(lst < n_lst - 1)
            def _():
                halo_copy(g, c).start()

            vis_copy(g, c).start()

    trig(0)
    for g in range(GROUPS):
        for d in range(1, chips):
            multiply(g, d)
        multiply(g, 0)
        if g < GROUPS - 1:
            trig(g + 1)
        forward(g)
        if g == 0:
            spread_taps()
        if g >= 2:
            finish(g - 2)
    for g in range(max(GROUPS - 2, 0), GROUPS):
        finish(g)

    @pl.loop(0, GROUPS)
    def _(g):
        rows = group_rows(g)
        for q in range(chans):
            c = channel_at(q)

            @pl.when(lst > 0)
            def _():
                halo_copy(g, c).wait_recv()

            for r in range(2):
                total = jnp.dot(tail[c, r, rows, :], toep[c, :TAIL, :], preferred_element_type=F32)
                total = total + jnp.dot(vis[c, r, rows, :], toep[c, TAIL:, :], preferred_element_type=F32)
                out[c, r, rows, :] = total.astype(BF16)
            out_copy(g, c).start()

    @pl.loop(0, GROUPS)
    def _(g):
        for d in range(chips):
            pair_copy(g, d).wait_send()
        for c in range(chans):
            for d in range(1, chips):
                far_copy(g, d, c).wait_send()

            @pl.when(lst < n_lst - 1)
            def _():
                halo_copy(g, c).wait_send()

            vis_copy(g, c).wait()
            out_copy(g, c).wait()


def shards(n_freq, n_lst, sky_east, sky_north, sky_flux, sky_scint, visible, antenna_coords, baseline_antennas, filter_taps):
    chans = filter_taps.shape[0]
    local_src, times = sky_scint.shape
    count = baseline_antennas.shape[0]
    group = count // GROUPS
    chips = n_freq // 2
    n_chan = chans * n_freq
    shape = jax.ShapeDtypeStruct((chans, 2, count, times), BF16)
    vmem = pl.BlockSpec(memory_space=pltpu.VMEM)
    hbm = pl.BlockSpec(memory_space=pl.ANY)
    dma = pltpu.SemaphoreType.DMA
    far = max(chips - 1, 1)
    rows = (local_src // 128, 128)
    return pl.pallas_call(
        functools.partial(kernel, (n_freq, n_lst, chans)),
        out_shape=(shape, shape),
        in_specs=[vmem] * 7 + [hbm],
        out_specs=(hbm, hbm),
        scratch_shapes=[
            pltpu.VMEM((local_src, times), BF16),
            pltpu.VMEM((chans, 2, count, times), BF16),
            pltpu.VMEM((chans, 2, count, times), BF16),
            pltpu.VMEM((ROWS, local_src), BF16),
            pltpu.VMEM((local_src, ROWS), BF16),
            pltpu.VMEM((ROWS, 2 * times), BF16),
            pltpu.VMEM((n_chan, 2 * group, local_src), BF16),
            pltpu.VMEM((n_chan, local_src, times), BF16),
            pltpu.VMEM((visible.shape[1], times), F32),
            pltpu.VMEM((GROUPS, 2 * group, ROWS), BF16),
            pltpu.VMEM((count, 128), F32),
            pltpu.VMEM((chans, TAIL + times, times), BF16),
            pltpu.VMEM((8, TAIL + times), F32),
            pltpu.VMEM((chans, 2, count, TAIL), BF16),
            pltpu.VMEM((GROUPS, chips, chans, 2 * group, times), F32),
            pltpu.VMEM((GROUPS, chips, chans, 2 * group, times), BF16),
            pltpu.VMEM((GROUPS, chips, chans, 2 * group, times), BF16),
            pltpu.VMEM((GROUPS, far, chans, 2 * group, times), BF16),
            pltpu.VMEM((GROUPS, chips, chans, 2 * group, times), BF16),
            dma,
            dma((GROUPS, chips)), dma((GROUPS, chips)),
            dma((GROUPS, far, chans)), dma((GROUPS, chips, chans)),
            dma((GROUPS, chans)), dma((GROUPS, chans)),
            dma((GROUPS, chans)), dma((GROUPS, chans)),
        ],
        compiler_params=pltpu.CompilerParams(
            collective_id=0, has_side_effects=True, vmem_limit_bytes=64000000
        ),
    )(
        sky_east.reshape(rows), sky_north.reshape(rows), sky_flux.reshape(rows),
        visible, antenna_coords.T, baseline_antennas.T, filter_taps, sky_scint,
    )


def solution(mesh):
    return jax.shard_map(
        functools.partial(shards, mesh.shape["freq"], mesh.shape["lst"]),
        mesh=mesh,
        in_specs=(
            P(("trial", "freq")),
            P(("trial", "freq")),
            P(("trial", "freq")),
            P(("trial", "freq"), "lst"),
            P(("trial", "lst"), None),
            P(),
            P(),
            P("freq", None),
        ),
        out_specs=(
            P(("trial", "freq"), None, None, "lst"),
            P(("trial", "freq"), None, None, "lst"),
        ),
        check_vma=False,
    )
```

```python
import functools
import math

import jax
import jax.numpy as jnp
import numpy as np
from jax import lax
from jax.experimental import pallas as pl
from jax.experimental.pallas import tpu as pltpu
from jax.sharding import PartitionSpec as P

SRC_BLOCK = 128
TAIL = 256
BLOCK_T = 8

C_LIGHT = 299792458.0
NU_START = 150000000.0
NU_STEP = 97656.25
OMEGA_STEP = 4.37526e-05
BEAM_SIGMA = 0.35
CENTRE_START = -0.045
LOG2E = math.log2(math.e)
ROUNDER = 1.5 * 2.0**23
ROWS = 16
GROUPS = 4
PARTS = 2
TILE = 256
FIRST_TILE = 512
AMP_TILE = 32
AMP_STEP = 256
MESH = pl.DeviceIdType.MESH
F32 = jnp.float32
BF16 = jnp.bfloat16


def fit_even(fun, reach, degree):
    nodes = np.cos((np.arange(400) + 0.5) * np.pi / 400)
    z = 0.5 * reach * reach * (nodes + 1.0)
    cheb = np.polynomial.chebyshev.Chebyshev.fit(z, fun(np.sqrt(z)), degree, domain=[0.0, reach * reach])
    return [float(c) for c in cheb.convert(kind=np.polynomial.Polynomial).coef]


def cos_turn(x):
    return np.cos(2.0 * np.pi * x)


def sin_turn(x):
    return np.sin(2.0 * np.pi * x) / x


COS_FULL = fit_even(cos_turn, 0.5, 5)
SIN_FULL = fit_even(sin_turn, 0.5, 4)
STEP_REACH = 0.12
COS_STEP = fit_even(cos_turn, STEP_REACH, 3)
SIN_STEP = fit_even(sin_turn, STEP_REACH, 2)


def horner(coefs, z):
    total = coefs[-1] * z + coefs[-2]
    for c in coefs[-3::-1]:
        total = total * z + c
    return total


def cos_minus_sin(turns):
    r = turns - ((turns + ROUNDER) - ROUNDER)
    z = r * r
    return horner(COS_FULL, z), horner([-c for c in SIN_FULL], z) * r


def sincos_turns(turns):
    r = turns - ((turns + ROUNDER) - ROUNDER)
    z = r * r
    return horner(COS_FULL, z), horner(SIN_FULL, z) * r


def sincos_step(r):
    z = r * r
    return horner(COS_STEP, z), horner(SIN_STEP, z) * r


def pieces(x):
    high = x.astype(BF16).astype(F32)
    middle = (x - high).astype(BF16).astype(F32)
    low = (x - high - middle).astype(BF16).astype(F32)
    return high, middle, low


def rowdot(a, b):
    return lax.dot_general(a, b, (((0,), (0,)), ((), ())), preferred_element_type=F32)


def kernel(
    dims,
    east_hbm, north_hbm, flux_hbm, visible_hbm, coords_hbm, pairs_hbm, taps_hbm, scint_hbm,
    vis, out,
    east_ref, north_ref, flux_ref, visible_ref, coords_ref, pairs_ref, taps_ref,
    scint, phase_rows, beam_cols, beam_right, planes_even, planes_odd, amps, mask_rows, coefs, lines, toep, tap_rows, tail,
    far_totals, own_totals, pair_out, pair_in, far_out, far_in,
    in_sems, pair_send, pair_recv, far_send, far_recv, halo_send, halo_recv,
):
    n_freq, n_lst, chans = dims
    local_src, times = scint.shape
    count = pairs_ref.shape[1]
    group = count // GROUPS
    part = group // PARTS
    chips = n_freq // 2
    per_chip = 2 * chans
    n_chan = chips * per_chip
    total_src = local_src * n_freq
    blocks = local_src // SRC_BLOCK
    me = lax.axis_index("freq")
    lst = lax.axis_index("lst")
    chip, core = me // 2, me % 2
    partner = chip * 2 + (1 - core)

    loads = [
        pltpu.make_async_copy(src, dst, in_sems.at[i])
        for i, (src, dst) in enumerate((
            (east_hbm, east_ref), (north_hbm, north_ref), (flux_hbm, flux_ref), (coords_hbm, coords_ref),
            (pairs_hbm, pairs_ref), (visible_hbm, visible_ref), (scint_hbm, scint), (taps_hbm, taps_ref),
        ))
    ]
    for load in loads:
        load.start()

    barrier = pltpu.get_barrier_semaphore()
    pl.semaphore_signal(barrier, inc=1, device_id={"freq": partner}, device_id_type=MESH)
    for d in range(1, chips):
        pl.semaphore_signal(
            barrier, inc=1, device_id={"freq": ((chip + d) % chips) * 2 + core}, device_id_type=MESH
        )

    @pl.when(lst > 0)
    def _():
        pl.semaphore_signal(barrier, inc=1, device_id={"lst": lst - 1}, device_id_type=MESH)

    def send(src, dst, ssem, rsem, to):
        return pltpu.make_async_remote_copy(
            src_ref=src, dst_ref=dst, send_sem=ssem, recv_sem=rsem, device_id=to, device_id_type=MESH
        )

    rising = chip * 2 >= chips
    way = jnp.where(rising, 1, -1)
    way_f = way.astype(F32)
    first = jnp.where(rising, 0, n_chan - 1).astype(F32)
    nu_first = NU_START + NU_STEP * first
    own_place = jnp.where(rising, chip, chips - 1 - chip)
    own_half = jnp.where(rising, core, 1 - core)
    nus = [NU_START + NU_STEP * (me * chans + c).astype(F32) for c in range(chans)]

    def place_of(d):
        return (own_place + d) % chips

    def chip_at(d):
        place = place_of(d)
        return jnp.where(rising, place, chips - 1 - place)

    def channel_at(q):
        return jnp.where(rising, q, chans - 1 - q)

    samples = (lst * times + lax.broadcasted_iota(jnp.int32, (1, times), 1)).astype(F32)
    centre = CENTRE_START + OMEGA_STEP * samples
    row_id = lax.broadcasted_iota(jnp.int32, (ROWS, times), 0)
    delta = NU_STEP / NU_START
    broad = 0.5 * LOG2E / (BEAM_SIGMA * BEAM_SIGMA)
    ratio = nu_first * (1.0 / NU_START)
    half = broad * ratio * ratio
    slope = broad * delta * way_f * (2.0 * ratio + delta * way_f)
    bend = 2.0 * broad * delta * delta / slope
    for at, scale, offset in ((0, half, 3), (1, slope, 9)):
        table = jnp.where((row_id >= offset) & (row_id < offset + 3), 1.0, 0.0)
        for base, rows in ((0, pieces(centre * (2.0 * scale))), (6, pieces(centre * centre * (-scale)))):
            for i, row in enumerate(rows):
                table = jnp.where(row_id == base + i, row, table)
        beam_right[:, at * times : (at + 1) * times] = table.astype(BF16)

    for load in loads[:3]:
        load.wait()
    l_all = east_ref[...].astype(F32)
    m_all = north_ref[...].astype(F32)
    radius = l_all * l_all + m_all * m_all
    level = jnp.log(flux_ref[...].astype(F32) * (1.0 / math.sqrt(total_src))) * LOG2E - radius * half
    level_rows = pieces(level)
    slope_rows = pieces(radius * (-slope))
    src_row = lax.broadcasted_iota(jnp.int32, (ROWS, SRC_BLOCK), 0)
    for k in range(blocks):
        at = slice(k, k + 1)
        rows = slice(k * SRC_BLOCK, (k + 1) * SRC_BLOCK)
        l = l_all[at]
        phase_rows[:, rows] = jnp.where(src_row < 3, l, jnp.where(src_row < 6, m_all[at], 0.0)).astype(BF16)
        table = jnp.where(src_row < 3, l, jnp.where(src_row < 9, 1.0, 0.0))
        for base, values in ((3, level_rows), (9, slope_rows)):
            for i, value in enumerate(values):
                table = jnp.where(src_row == base + i, value[at], table)
        beam_cols[rows, :] = table.T.astype(BF16)

    for load in loads[3:6]:
        load.wait()
    antennas = coords_ref.shape[1]
    ids = lax.broadcasted_iota(jnp.int32, (antennas, count), 0)
    select = ((pairs_ref[0:1, :] == ids).astype(F32) - (pairs_ref[1:2, :] == ids).astype(F32)).astype(BF16)
    place = jnp.concatenate([*pieces(coords_ref[...]), jnp.zeros((2, antennas), F32)], axis=0)
    picked = jnp.dot(place.astype(BF16), select, preferred_element_type=F32)
    both = (picked[4:6, :] + picked[2:4, :]) + picked[0:2, :]
    pair_row = lax.broadcasted_iota(jnp.int32, (ROWS, count), 0)

    def coef_rows(scale):
        table = jnp.where(pair_row == 6, both[0:1, :], 0.0)
        for base in range(2):
            for i, piece in enumerate(pieces(both[base : base + 1, :] * scale)):
                table = jnp.where(pair_row == 3 * base + i, piece, table)
        return table.T

    main = coef_rows(nu_first * (1.0 / C_LIGHT))
    step = coef_rows(way_f * (NU_STEP / C_LIGHT)).astype(BF16)
    lines[...] = main
    main = main.astype(BF16)
    for g in range(GROUPS):
        coefs[g, 0:group, :] = main[g * group : (g + 1) * group]
        coefs[g, group : 2 * group, :] = step[g * group : (g + 1) * group]

    t_blocks = visible_ref.shape[0]
    spread = (
        lax.broadcasted_iota(jnp.int32, (t_blocks, times), 1) // BLOCK_T
        == lax.broadcasted_iota(jnp.int32, (t_blocks, times), 0)
    ).astype(BF16)
    mask_rows[...] = rowdot(visible_ref[...].astype(F32).astype(BF16), spread)

    loads[6].wait()
    loads[7].wait()

    def amplitudes(start, end):
        @pl.loop(0, local_src // AMP_STEP)
        def _(i):
            for k in range(AMP_STEP // AMP_TILE):
                rows = pl.ds(pl.multiple_of(i * AMP_STEP + k * AMP_TILE, AMP_TILE), AMP_TILE)
                power = jnp.dot(beam_cols[rows, :], beam_right[...], preferred_element_type=F32)
                block = i * (AMP_STEP // SRC_BLOCK) + k // (SRC_BLOCK // AMP_TILE)
                mask = mask_rows[pl.ds(me * blocks + block, 1), :]
                log_value, log_gain = power[:, :times], power[:, times:]
                log_change = log_gain * bend
                if start > 0:
                    log_value = log_value + log_gain * (start + (0.5 * start * (start - 1)) * bend)
                    log_gain = log_gain + log_change * start
                value = jnp.exp2(log_value) * (scint[rows, :].astype(F32) * mask)
                gain = jnp.exp2(log_gain)
                change = jnp.exp2(log_change)
                for p in range(start, end):
                    amps[p, rows, :] = value.astype(BF16)
                    if p < end - 1:
                        value = value * gain
                    if p < end - 2:
                        gain = gain * change

    planes = (planes_even, planes_odd)

    def trig_tile(g, cols, start, end):
        turns = jnp.dot(coefs[g], phase_rows[:, cols], preferred_element_type=F32)
        if start > 0:
            co, si = cos_minus_sin(turns[:group] + turns[group:] * start)
        else:
            co, si = cos_minus_sin(turns[:group])
        cd, sd = sincos_step(turns[group:])
        twice = cd + cd
        older = None
        for p in range(start, end):
            planes[g % 2][p, 0:group, cols] = co.astype(BF16)
            planes[g % 2][p, group : 2 * group, cols] = si.astype(BF16)
            if p == start:
                older, (co, si) = (co, si), (co * cd + si * sd, si * cd - co * sd)
            else:
                older, (co, si) = (co, si), (twice * co - older[0], twice * si - older[1])

    def trig_first(start, end):
        @pl.loop(0, local_src // FIRST_TILE)
        def _(i):
            trig_tile(0, pl.ds(pl.multiple_of(i * FIRST_TILE, FIRST_TILE), FIRST_TILE), start, end)

    def partial_sum(g, d, half, q):
        p = place_of(d) * per_chip + half * chans + q
        return jnp.dot(planes[g % 2][p], amps[p], preferred_element_type=F32)

    def pair_copy(g, d):
        return send(pair_out.at[g, d], pair_in.at[g, d], pair_send.at[g, d], pair_recv.at[g, d], {"freq": partner})

    def far_copy(g, d, c, h):
        rows = pl.ds(h * part, part)
        return send(
            far_out.at[g, d - 1, c, :, rows, :], far_in.at[g, chip, c, :, rows, :],
            far_send.at[g, d - 1, c, h], far_recv.at[g, chip, c, h], {"freq": chip_at(d) * 2 + core},
        )

    def far_arrival(g, d, c, h):
        src = (chip + d) % chips
        block = far_in.at[g, src, c, :, pl.ds(h * part, part), :]
        return send(block, block, far_send.at[g, d - 1, c, h], far_recv.at[g, src, c, h], {"freq": src * 2 + core})

    def part_rows(g, h):
        at = g * group + h * part
        return pl.ds(at if isinstance(at, int) else pl.multiple_of(at, part), part)

    def halo_copy(g, c, h):
        rows = part_rows(g, h)
        return send(
            vis.at[c, :, rows, :], tail.at[c, :, rows, :], halo_send.at[g, c, h], halo_recv.at[g, c, h],
            {"lst": (lst + 1) % n_lst},
        )

    pl.semaphore_wait(barrier, chips + (lst < n_lst - 1).astype(jnp.int32))

    @pl.when(lst == 0)
    def _():
        tail[...] = jnp.zeros_like(tail)

    def kept_totals(g, d):
        return own_totals.at[g] if d == 0 else far_totals.at[g % 2, d - 1]

    def multiply(g, d, kept):
        for q in range(chans):
            if kept:
                kept_totals(g, d)[q] = partial_sum(g, d, own_half, q)
            else:
                pair_out[g, d, q] = partial_sum(g, d, 1 - own_half, q).astype(BF16)
        if not kept:
            pair_copy(g, d).start()

    def forward(g):
        for d in range(1, chips):
            pair_copy(g, d).wait_recv()
            for h in range(PARTS):
                for q in range(chans):
                    c = channel_at(q)
                    for r in range(2):
                        rows = slice(r * group + h * part, r * group + (h + 1) * part)
                        added = far_totals[g % 2, d - 1, q, rows, :] + pair_in[g, d, q, rows, :].astype(F32)
                        far_out[g, d - 1, c, r, h * part : (h + 1) * part, :] = added.astype(BF16)
                    far_copy(g, d, c, h).start()

    def spread_taps():
        tap_rows[...] = jnp.zeros_like(tap_rows)
        tap_rows[0:chans, 0 : TAIL + 1] = taps_ref[...].astype(F32)
        for c in range(chans):
            wide = jnp.broadcast_to(tap_rows[c : c + 1, :], (TAIL + times, TAIL + times))
            skewed = pltpu.roll(wide, 0, 1, stride=1, stride_axis=0)
            toep[c] = skewed[:, TAIL:].astype(BF16)

    def finish(g):
        pair_copy(g, 0).wait_recv()
        for h in range(PARTS):
            rows = part_rows(g, h)
            for q in range(chans):
                c = channel_at(q)
                for d in range(1, chips):
                    far_arrival(g, d, c, h).wait_recv()
                real, imag = [
                    sum(
                        (far_in[g, (chip + d) % chips, c, r, h * part : (h + 1) * part, :].astype(F32) for d in range(1, chips)),
                        start=own_totals[g, q, at, :] + pair_in[g, 0, q, at, :].astype(F32),
                    )
                    for r, at in enumerate(
                        slice(r * group + h * part, r * group + (h + 1) * part) for r in range(2)
                    )
                ]
                scale = (NU_START + NU_STEP * (me * chans + c).astype(F32)) * (OMEGA_STEP / C_LIGHT)
                co, si = sincos_turns((lines[rows, 6:7] * scale) * samples)
                vis[c, 0, rows, :] = (co * real + si * imag).astype(BF16)
                vis[c, 1, rows, :] = (co * imag - si * real).astype(BF16)

                @pl.when(lst < n_lst - 1)
                def _():
                    halo_copy(g, c, h).start()


    def smooth(g):
        for h in range(PARTS):
            rows = part_rows(g, h)
            for q in range(chans):
                c = channel_at(q)

                @pl.when(lst > 0)
                def _():
                    halo_copy(g, c, h).wait_recv()

                for r in range(2):
                    total = jnp.dot(tail[c, r, rows, :], toep[c, :TAIL, :], preferred_element_type=F32)
                    total = total + jnp.dot(vis[c, r, rows, :], toep[c, TAIL:, :], preferred_element_type=F32)
                    out[c, r, rows, :] = total.astype(BF16)

    tiles = local_src // TILE

    def multiply_beside(g, stages, new):
        for i in range(max(tiles, len(stages))):
            if i < len(stages):
                multiply(g, *stages[i])
            if i < tiles and new < GROUPS:
                trig_tile(new, slice(i * TILE, (i + 1) * TILE), 0, n_chan)

    far_stages = [(d, kept) for d in range(1, chips) for kept in (False, True)]
    own_stages = [(0, False), (0, True)]
    middle = n_chan // 2 if chips == 2 else n_chan
    amplitudes(0, middle)
    trig_first(0, middle)
    for stage in far_stages:
        multiply(0, *stage)
    if middle < n_chan:
        amplitudes(middle, n_chan)
    forward(0)
    if middle < n_chan:
        trig_first(middle, n_chan)
    multiply_beside(0, own_stages, 1)
    for g in range(1, GROUPS):
        multiply_beside(g, far_stages + own_stages, g + 1)
        forward(g)
        if g == 1:
            finish(0)
        if g == GROUPS - 1:
            spread_taps()
    for g in range(1, GROUPS):
        finish(g)
        smooth(g - 1)
    smooth(GROUPS - 1)

    @pl.loop(0, GROUPS)
    def _(g):
        for d in range(chips):
            pair_copy(g, d).wait_send()
        for c in range(chans):
            for h in range(PARTS):
                for d in range(1, chips):
                    far_copy(g, d, c, h).wait_send()

                @pl.when(lst < n_lst - 1)
                def _():
                    halo_copy(g, c, h).wait_send()


def leave(vis, out, vis_hbm, out_hbm, sems):
    copies = [
        pltpu.make_async_copy(src.at[c, r], dst.at[c, r], sems.at[i, c, r])
        for i, (src, dst) in enumerate(((vis, vis_hbm), (out, out_hbm)))
        for c in range(vis.shape[0])
        for r in range(2)
    ]
    for copy in copies:
        copy.start()
    for copy in copies:
        copy.wait()


def shards(n_freq, n_lst, sky_east, sky_north, sky_flux, sky_scint, visible, antenna_coords, baseline_antennas, filter_taps):
    chans = filter_taps.shape[0]
    local_src, times = sky_scint.shape
    count = baseline_antennas.shape[0]
    group = count // GROUPS
    chips = n_freq // 2
    n_chan = chans * n_freq
    held = pltpu.VMEM((chans, 2, count, times), BF16)
    shape = jax.ShapeDtypeStruct((chans, 2, count, times), BF16)
    vmem = pl.BlockSpec(memory_space=pltpu.VMEM)
    hbm = pl.BlockSpec(memory_space=pl.ANY)
    dma = pltpu.SemaphoreType.DMA
    far = max(chips - 1, 1)
    rows = (local_src // 128, 128)
    vis, out = pl.pallas_call(
        functools.partial(kernel, (n_freq, n_lst, chans)),
        out_shape=(held, held),
        in_specs=[hbm] * 8,
        out_specs=(vmem, vmem),
        scratch_shapes=[
            pltpu.VMEM(rows, BF16), pltpu.VMEM(rows, BF16), pltpu.VMEM(rows, BF16),
            pltpu.VMEM(visible.shape, jnp.int32),
            pltpu.VMEM(antenna_coords.T.shape, F32),
            pltpu.VMEM(baseline_antennas.T.shape, jnp.int32),
            pltpu.VMEM(filter_taps.shape, BF16),
            pltpu.VMEM((local_src, times), BF16),
            pltpu.VMEM((ROWS, local_src), BF16),
            pltpu.VMEM((local_src, ROWS), BF16),
            pltpu.VMEM((ROWS, 2 * times), BF16),
            pltpu.VMEM((n_chan, 2 * group, local_src), BF16),
            pltpu.VMEM((n_chan, 2 * group, local_src), BF16),
            pltpu.VMEM((n_chan, local_src, times), BF16),
            pltpu.VMEM((visible.shape[1], times), F32),
            pltpu.VMEM((GROUPS, 2 * group, ROWS), BF16),
            pltpu.VMEM((count, ROWS), F32),
            pltpu.VMEM((chans, TAIL + times, times), BF16),
            pltpu.VMEM((8, TAIL + times), F32),
            pltpu.VMEM((chans, 2, count, TAIL), BF16),
            pltpu.VMEM((2, far, chans, 2 * group, times), F32),
            pltpu.VMEM((GROUPS, chans, 2 * group, times), F32),
            pltpu.VMEM((GROUPS, chips, chans, 2 * group, times), BF16),
            pltpu.VMEM((GROUPS, chips, chans, 2 * group, times), BF16),
            pltpu.VMEM((GROUPS, far, chans, 2, group, times), BF16),
            pltpu.VMEM((GROUPS, chips, chans, 2, group, times), BF16),
            dma((8,)),
            dma((GROUPS, chips)), dma((GROUPS, chips)),
            dma((GROUPS, far, chans, PARTS)), dma((GROUPS, chips, chans, PARTS)),
            dma((GROUPS, chans, PARTS)), dma((GROUPS, chans, PARTS)),
        ],
        compiler_params=pltpu.CompilerParams(
            collective_id=0, has_side_effects=True, vmem_limit_bytes=64000000
        ),
    )(
        sky_east.reshape(rows), sky_north.reshape(rows), sky_flux.reshape(rows),
        visible, antenna_coords.T, baseline_antennas.T, filter_taps, sky_scint,
    )
    return pl.pallas_call(
        leave,
        out_shape=(shape, shape),
        in_specs=[vmem, vmem],
        out_specs=(hbm, hbm),
        scratch_shapes=[dma((2, chans, 2))],
        compiler_params=pltpu.CompilerParams(vmem_limit_bytes=1 << 20),
    )(vis, out)


def solution(mesh):
    return jax.shard_map(
        functools.partial(shards, mesh.shape["freq"], mesh.shape["lst"]),
        mesh=mesh,
        in_specs=(
            P(("trial", "freq")),
            P(("trial", "freq")),
            P(("trial", "freq")),
            P(("trial", "freq"), "lst"),
            P(("trial", "lst"), None),
            P(),
            P(),
            P("freq", None),
        ),
        out_specs=(
            P(("trial", "freq"), None, None, "lst"),
            P(("trial", "freq"), None, None, "lst"),
        ),
        check_vma=False,
    )
```

```python
import functools
import math

import jax
import jax.numpy as jnp
import numpy as np
from jax import lax
from jax.experimental import pallas as pl
from jax.experimental.pallas import tpu as pltpu
from jax.sharding import PartitionSpec as P

SRC_BLOCK = 128
TAIL = 256
BLOCK_T = 8

C_LIGHT = 299792458.0
NU_START = 150000000.0
NU_STEP = 97656.25
OMEGA_STEP = 4.37526e-05
BEAM_SIGMA = 0.35
CENTRE_START = -0.045
LOG2E = math.log2(math.e)
ROUNDER = 1.5 * 2.0**23
ROWS = 16
GROUPS = 4
PARTS = 2
TILE = 256
FIRST_TILE = 1024
AMP_TILE = 32
AMP_STEP = 1024
MESH = pl.DeviceIdType.MESH
F32 = jnp.float32
BF16 = jnp.bfloat16


def fit_even(fun, reach, degree):
    nodes = np.cos((np.arange(400) + 0.5) * np.pi / 400)
    z = 0.5 * reach * reach * (nodes + 1.0)
    cheb = np.polynomial.chebyshev.Chebyshev.fit(z, fun(np.sqrt(z)), degree, domain=[0.0, reach * reach])
    return [float(c) for c in cheb.convert(kind=np.polynomial.Polynomial).coef]


def cos_turn(x):
    return np.cos(2.0 * np.pi * x)


def sin_turn(x):
    return np.sin(2.0 * np.pi * x) / x


COS_FULL = fit_even(cos_turn, 0.5, 5)
SIN_FULL = fit_even(sin_turn, 0.5, 4)
STEP_REACH = 0.12
COS_STEP = fit_even(cos_turn, STEP_REACH, 3)
SIN_STEP = fit_even(sin_turn, STEP_REACH, 2)


def horner(coefs, z):
    total = coefs[-1] * z + coefs[-2]
    for c in coefs[-3::-1]:
        total = total * z + c
    return total


def cos_minus_sin(turns):
    r = turns - ((turns + ROUNDER) - ROUNDER)
    z = r * r
    return horner(COS_FULL, z), horner([-c for c in SIN_FULL], z) * r


def sincos_turns(turns):
    r = turns - ((turns + ROUNDER) - ROUNDER)
    z = r * r
    return horner(COS_FULL, z), horner(SIN_FULL, z) * r


def sincos_step(r):
    z = r * r
    return horner(COS_STEP, z), horner(SIN_STEP, z) * r


def pieces(x):
    high = x.astype(BF16).astype(F32)
    middle = (x - high).astype(BF16).astype(F32)
    low = (x - high - middle).astype(BF16).astype(F32)
    return high, middle, low


def rowdot(a, b):
    return lax.dot_general(a, b, (((0,), (0,)), ((), ())), preferred_element_type=F32)


def kernel(
    dims,
    east_hbm, north_hbm, flux_hbm, visible_hbm, coords_hbm, pairs_hbm, taps_hbm, scint_hbm,
    vis, out,
    east_ref, north_ref, flux_ref, visible_ref, coords_ref, pairs_ref, taps_ref,
    scint, phase_rows, beam_cols, beam_right, far_even, far_odd, own_even, own_odd, state, amps, mask_rows, coefs, lines, toep, tap_rows, tail,
    far_totals, own_totals, pair_out, pair_in, far_out, far_in,
    in_sems, pair_send, pair_recv, far_send, far_recv, halo_send, halo_recv,
):
    n_freq, n_lst, chans = dims
    local_src, times = scint.shape
    count = pairs_ref.shape[1]
    group = count // GROUPS
    part = group // PARTS
    chips = n_freq // 2
    per_chip = 2 * chans
    n_chan = chips * per_chip
    total_src = local_src * n_freq
    blocks = local_src // SRC_BLOCK
    me = lax.axis_index("freq")
    lst = lax.axis_index("lst")
    chip, core = me // 2, me % 2
    partner = chip * 2 + (1 - core)

    loads = [
        pltpu.make_async_copy(src, dst, in_sems.at[i])
        for i, (src, dst) in enumerate((
            (east_hbm, east_ref), (north_hbm, north_ref), (flux_hbm, flux_ref), (coords_hbm, coords_ref),
            (pairs_hbm, pairs_ref), (visible_hbm, visible_ref), (scint_hbm, scint), (taps_hbm, taps_ref),
        ))
    ]
    for load in loads:
        load.start()

    barrier = pltpu.get_barrier_semaphore()
    pl.semaphore_signal(barrier, inc=1, device_id={"freq": partner}, device_id_type=MESH)
    for d in range(1, chips):
        pl.semaphore_signal(
            barrier, inc=1, device_id={"freq": ((chip + d) % chips) * 2 + core}, device_id_type=MESH
        )

    @pl.when(lst > 0)
    def _():
        pl.semaphore_signal(barrier, inc=1, device_id={"lst": lst - 1}, device_id_type=MESH)

    def send(src, dst, ssem, rsem, to):
        return pltpu.make_async_remote_copy(
            src_ref=src, dst_ref=dst, send_sem=ssem, recv_sem=rsem, device_id=to, device_id_type=MESH
        )

    rising = chip * 2 >= chips
    way = jnp.where(rising, 1, -1)
    way_f = way.astype(F32)
    first = jnp.where(rising, 0, n_chan - 1).astype(F32)
    nu_first = NU_START + NU_STEP * first
    own_place = jnp.where(rising, chip, chips - 1 - chip)
    own_half = jnp.where(rising, core, 1 - core)
    nus = [NU_START + NU_STEP * (me * chans + c).astype(F32) for c in range(chans)]

    def place_of(d):
        return (own_place + d) % chips

    def chip_at(d):
        place = place_of(d)
        return jnp.where(rising, place, chips - 1 - place)

    def channel_at(q):
        return jnp.where(rising, q, chans - 1 - q)

    samples = (lst * times + lax.broadcasted_iota(jnp.int32, (1, times), 1)).astype(F32)
    centre = CENTRE_START + OMEGA_STEP * samples
    row_id = lax.broadcasted_iota(jnp.int32, (ROWS, times), 0)
    delta = NU_STEP / NU_START
    broad = 0.5 * LOG2E / (BEAM_SIGMA * BEAM_SIGMA)
    ratio = nu_first * (1.0 / NU_START)
    half = broad * ratio * ratio
    slope = broad * delta * way_f * (2.0 * ratio + delta * way_f)
    bend = 2.0 * broad * delta * delta / slope
    for at, scale, offset in ((0, half, 3), (1, slope, 9)):
        table = jnp.where((row_id >= offset) & (row_id < offset + 3), 1.0, 0.0)
        for base, rows in ((0, pieces(centre * (2.0 * scale))), (6, pieces(centre * centre * (-scale)))):
            for i, row in enumerate(rows):
                table = jnp.where(row_id == base + i, row, table)
        beam_right[:, at * times : (at + 1) * times] = table.astype(BF16)

    for load in loads[:6]:
        load.wait()
    l_all = east_ref[...].astype(F32)
    m_all = north_ref[...].astype(F32)
    radius = l_all * l_all + m_all * m_all
    level = jnp.log(flux_ref[...].astype(F32) * (1.0 / math.sqrt(total_src))) * LOG2E - radius * half
    level_rows = pieces(level)
    slope_rows = pieces(radius * (-slope))
    src_row = lax.broadcasted_iota(jnp.int32, (ROWS, SRC_BLOCK), 0)
    for k in range(blocks):
        at = slice(k, k + 1)
        rows = slice(k * SRC_BLOCK, (k + 1) * SRC_BLOCK)
        l = l_all[at]
        phase_rows[:, rows] = jnp.where(src_row < 3, l, jnp.where(src_row < 6, m_all[at], 0.0)).astype(BF16)
        table = jnp.where(src_row < 3, l, jnp.where(src_row < 9, 1.0, 0.0))
        for base, values in ((3, level_rows), (9, slope_rows)):
            for i, value in enumerate(values):
                table = jnp.where(src_row == base + i, value[at], table)
        beam_cols[rows, :] = table.T.astype(BF16)

    antennas = coords_ref.shape[1]
    ids = lax.broadcasted_iota(jnp.int32, (antennas, count), 0)
    select = ((pairs_ref[0:1, :] == ids).astype(F32) - (pairs_ref[1:2, :] == ids).astype(F32)).astype(BF16)
    place = jnp.concatenate([*pieces(coords_ref[...]), jnp.zeros((2, antennas), F32)], axis=0)
    picked = jnp.dot(place.astype(BF16), select, preferred_element_type=F32)
    both = (picked[4:6, :] + picked[2:4, :]) + picked[0:2, :]
    pair_row = lax.broadcasted_iota(jnp.int32, (ROWS, count), 0)

    def coef_rows(scale):
        table = jnp.where(pair_row == 6, both[0:1, :], 0.0)
        for base in range(2):
            for i, piece in enumerate(pieces(both[base : base + 1, :] * scale)):
                table = jnp.where(pair_row == 3 * base + i, piece, table)
        return table.T

    main = coef_rows(nu_first * (1.0 / C_LIGHT))
    step = coef_rows(way_f * (NU_STEP / C_LIGHT)).astype(BF16)
    lines[...] = main
    main = main.astype(BF16)
    for g in range(GROUPS):
        coefs[g, 0:group, :] = main[g * group : (g + 1) * group]
        coefs[g, group : 2 * group, :] = step[g * group : (g + 1) * group]

    t_blocks = visible_ref.shape[0]
    spread = (
        lax.broadcasted_iota(jnp.int32, (t_blocks, times), 1) // BLOCK_T
        == lax.broadcasted_iota(jnp.int32, (t_blocks, times), 0)
    ).astype(BF16)
    mask_rows[...] = rowdot(visible_ref[...].astype(F32).astype(BF16), spread)

    loads[6].wait()

    def amplitudes(start, end):
        @pl.loop(0, local_src // AMP_STEP)
        def _(i):
            for k in range(AMP_STEP // AMP_TILE):
                rows = pl.ds(pl.multiple_of(i * AMP_STEP + k * AMP_TILE, AMP_TILE), AMP_TILE)
                power = jnp.dot(beam_cols[rows, :], beam_right[...], preferred_element_type=F32)
                block = i * (AMP_STEP // SRC_BLOCK) + k // (SRC_BLOCK // AMP_TILE)
                mask = mask_rows[pl.ds(me * blocks + block, 1), :]
                log_value, log_gain = power[:, :times], power[:, times:]
                log_change = log_gain * bend
                if start > 0:
                    log_value = log_value + log_gain * (start + (0.5 * start * (start - 1)) * bend)
                    log_gain = log_gain + log_change * start
                value = jnp.exp2(log_value) * (scint[rows, :].astype(F32) * mask)
                gain = jnp.exp2(log_gain)
                change = jnp.exp2(log_change)
                for p in range(start, end):
                    amps[p, rows, :] = value.astype(BF16)
                    if p < end - 1:
                        value = value * gain
                    if p < end - 2:
                        gain = gain * change

    split = chips == 2
    middle = n_chan // 2 if split else n_chan
    planes = ((far_even, own_even), (far_odd, own_odd))

    def keep_planes(g, later, p, cols, co, si):
        planes[g % 2][later][p, 0:group, cols] = co.astype(BF16)
        planes[g % 2][later][p, group : 2 * group, cols] = si.astype(BF16)

    def turn_on(g, later, p, cols, co, si, cd, sd, number):
        twice = cd + cd
        older = None
        for i in range(number):
            keep_planes(g, later, p + i, cols, co, si)
            if i == number - 1:
                break
            if older is None:
                older, (co, si) = (co, si), (co * cd + si * sd, si * cd - co * sd)
            else:
                older, (co, si) = (co, si), (twice * co - older[0], twice * si - older[1])
        return co, si

    def trig_far(g, cols):
        turns = jnp.dot(coefs[g], phase_rows[:, cols], preferred_element_type=F32)
        co, si = cos_minus_sin(turns[:group])
        cd, sd = sincos_step(turns[group:])
        co, si = turn_on(g, 0, 0, cols, co, si, cd, sd, middle)
        if split:
            for i, value in enumerate((co, si, cd, sd)):
                state[g % 2, i, :, cols] = value

    def trig_own(g, cols):
        co, si, cd, sd = [state[g % 2, i, :, cols] for i in range(4)]
        turn_on(g, 1, 0, cols, co * cd + si * sd, si * cd - co * sd, cd, sd, n_chan - middle)

    def trig_first():
        @pl.loop(0, local_src // FIRST_TILE)
        def _(i):
            trig_far(0, pl.ds(pl.multiple_of(i * FIRST_TILE, FIRST_TILE), FIRST_TILE))

    def partial_sum(g, d, half, q):
        if split:
            p = half * chans + q
            return jnp.dot(planes[g % 2][d == 0][p], amps[(d == 0) * middle + p], preferred_element_type=F32)
        p = place_of(d) * per_chip + half * chans + q
        return jnp.dot(planes[g % 2][0][p], amps[p], preferred_element_type=F32)

    def pair_copy(g, d, q):
        return send(
            pair_out.at[g, d, q], pair_in.at[g, d, q], pair_send.at[g, d, q], pair_recv.at[g, d, q], {"freq": partner}
        )

    def far_copy(g, d, c, h):
        rows = pl.ds(h * part, part)
        return send(
            far_out.at[g, d - 1, c, :, rows, :], far_in.at[g, chip, c, :, rows, :],
            far_send.at[g, d - 1, c, h], far_recv.at[g, chip, c, h], {"freq": chip_at(d) * 2 + core},
        )

    def far_arrival(g, d, c, h):
        src = (chip + d) % chips
        block = far_in.at[g, src, c, :, pl.ds(h * part, part), :]
        return send(block, block, far_send.at[g, d - 1, c, h], far_recv.at[g, src, c, h], {"freq": src * 2 + core})

    def group_rows(g):
        return pl.ds(g * group, group)

    def part_rows(g, h):
        at = g * group + h * part
        return pl.ds(at if isinstance(at, int) else pl.multiple_of(at, part), part)

    def halo_copy(g, c, h):
        rows = part_rows(g, h)
        return send(
            vis.at[c, :, rows, :], tail.at[c, :, rows, :], halo_send.at[g, c, h], halo_recv.at[g, c, h],
            {"lst": (lst + 1) % n_lst},
        )


    @pl.when(lst == 0)
    def _():
        tail[...] = jnp.zeros_like(tail)

    def kept_totals(g, d):
        return own_totals.at[g] if d == 0 else far_totals.at[g % 2, d - 1]

    def multiply(g, d, kept):
        for q in range(chans):
            if kept:
                kept_totals(g, d)[q] = partial_sum(g, d, own_half, q)
            else:
                pair_out[g, d, q] = partial_sum(g, d, 1 - own_half, q).astype(BF16)
                pair_copy(g, d, q).start()

    def forward(g):
        for d in range(1, chips):
            for q in range(chans):
                c = channel_at(q)
                pair_copy(g, d, q).wait_recv()
                for h in range(PARTS):
                    for r in range(2):
                        rows = slice(r * group + h * part, r * group + (h + 1) * part)
                        added = far_totals[g % 2, d - 1, q, rows, :] + pair_in[g, d, q, rows, :].astype(F32)
                        far_out[g, d - 1, c, r, h * part : (h + 1) * part, :] = added.astype(BF16)
                    far_copy(g, d, c, h).start()

    def spread_taps():
        loads[7].wait()
        tap_rows[...] = jnp.zeros_like(tap_rows)
        tap_rows[0:chans, 0 : TAIL + 1] = taps_ref[...].astype(F32)
        for c in range(chans):
            wide = jnp.broadcast_to(tap_rows[c : c + 1, :], (TAIL + times, TAIL + times))
            skewed = pltpu.roll(wide, 0, 1, stride=1, stride_axis=0)
            toep[c] = skewed[:, TAIL:].astype(BF16)

    def finish(g):
        for q in range(chans):
            c = channel_at(q)
            pair_copy(g, 0, q).wait_recv()
            for h in range(PARTS):
                rows = part_rows(g, h)
                for d in range(1, chips):
                    far_arrival(g, d, c, h).wait_recv()
                real, imag = [
                    sum(
                        (far_in[g, (chip + d) % chips, c, r, h * part : (h + 1) * part, :].astype(F32) for d in range(1, chips)),
                        start=own_totals[g, q, at, :] + pair_in[g, 0, q, at, :].astype(F32),
                    )
                    for r, at in enumerate(
                        slice(r * group + h * part, r * group + (h + 1) * part) for r in range(2)
                    )
                ]
                scale = (NU_START + NU_STEP * (me * chans + c).astype(F32)) * (OMEGA_STEP / C_LIGHT)
                co, si = sincos_turns((lines[rows, 6:7] * scale) * samples)
                vis[c, 0, rows, :] = (co * real + si * imag).astype(BF16)
                vis[c, 1, rows, :] = (co * imag - si * real).astype(BF16)

                @pl.when(lst < n_lst - 1)
                def _():
                    halo_copy(g, c, h).start()


    def smooth_own(g):
        rows = group_rows(g)
        for q in range(chans):
            c = channel_at(q)
            block = vis[c, :, rows, :].reshape(2 * group, times)
            own_totals[g, q] = jnp.dot(block, toep[c, TAIL:, :], preferred_element_type=F32)

    def smooth_tail(g, q, first, last):
        c = channel_at(q)
        for h in range(first, last):

            @pl.when(lst > 0)
            def _():
                halo_copy(g, c, h).wait_recv()

        size = (last - first) * part
        rows = pl.ds(g * group + first * part, size)
        block = tail[c, :, rows, :].reshape(2 * size, TAIL)
        total = jnp.dot(block, toep[c, :TAIL, :], preferred_element_type=F32)
        for r in range(2):
            own = own_totals[g, q, r * group + first * part : r * group + last * part, :]
            out[c, r, rows, :] = (total[r * size : (r + 1) * size] + own).astype(BF16)

    def smooth(g):
        for q in range(chans):
            smooth_tail(g, q, 0, PARTS)

    tiles = local_src // TILE

    def multiply_beside(g, stages, trig, new):
        for i in range(max(tiles, len(stages))):
            if i < len(stages):
                multiply(g, *stages[i])
            if i < tiles and trig is not None and new < GROUPS:
                trig(new, slice(i * TILE, (i + 1) * TILE))

    far_stages = [(d, kept) for d in range(1, chips) for kept in (False, True)]
    own_stages = [(0, False), (0, True)]
    own_trig = trig_own if split else None
    amplitudes(0, middle)
    trig_first()
    pl.semaphore_wait(barrier, chips + (lst < n_lst - 1).astype(jnp.int32))
    multiply_beside(0, far_stages, None, 0)
    if split:
        amplitudes(middle, n_chan)
    forward(0)
    for i in range(tiles):
        trig_far(1, slice(i * TILE, (i + 1) * TILE))
    for g in range(GROUPS):
        if g < GROUPS - 1:
            multiply_beside(g + 1, far_stages, own_trig, g)
        else:
            multiply_beside(g, [], own_trig, g)
        if split:
            multiply_beside(g, own_stages, trig_far, g + 2)
        else:
            multiply_beside(g, own_stages, None, 0)
            multiply_beside(g, [], trig_far, g + 2)
        if g < GROUPS - 1:
            forward(g + 1)
        if g > 1:
            smooth(g - 2)
        finish(g)
        if g == 0:
            spread_taps()
        smooth_own(g)
    smooth(GROUPS - 2)
    for q in range(chans):
        for h in range(PARTS):
            smooth_tail(GROUPS - 1, q, h, h + 1)

    @pl.loop(0, GROUPS)
    def _(g):
        for d in range(chips):
            for q in range(chans):
                pair_copy(g, d, q).wait_send()
        for c in range(chans):
            for h in range(PARTS):
                for d in range(1, chips):
                    far_copy(g, d, c, h).wait_send()

                @pl.when(lst < n_lst - 1)
                def _():
                    halo_copy(g, c, h).wait_send()


def leave(vis, out, vis_hbm, out_hbm, sems):
    copies = [
        pltpu.make_async_copy(src.at[c, r], dst.at[c, r], sems.at[i, c, r])
        for i, (src, dst) in enumerate(((vis, vis_hbm), (out, out_hbm)))
        for c in range(vis.shape[0])
        for r in range(2)
    ]
    for copy in copies:
        copy.start()
    for copy in copies:
        copy.wait()


def shards(n_freq, n_lst, sky_east, sky_north, sky_flux, sky_scint, visible, antenna_coords, baseline_antennas, filter_taps):
    chans = filter_taps.shape[0]
    local_src, times = sky_scint.shape
    count = baseline_antennas.shape[0]
    group = count // GROUPS
    chips = n_freq // 2
    n_chan = chans * n_freq
    held = pltpu.VMEM((chans, 2, count, times), BF16)
    shape = jax.ShapeDtypeStruct((chans, 2, count, times), BF16)
    vmem = pl.BlockSpec(memory_space=pltpu.VMEM)
    hbm = pl.BlockSpec(memory_space=pl.ANY)
    dma = pltpu.SemaphoreType.DMA
    far = max(chips - 1, 1)
    own = n_chan // 2 if chips == 2 else 0
    rows = (local_src // 128, 128)
    vis, out = pl.pallas_call(
        functools.partial(kernel, (n_freq, n_lst, chans)),
        out_shape=(held, held),
        in_specs=[hbm] * 8,
        out_specs=(vmem, vmem),
        scratch_shapes=[
            pltpu.VMEM(rows, BF16), pltpu.VMEM(rows, BF16), pltpu.VMEM(rows, BF16),
            pltpu.VMEM(visible.shape, jnp.int32),
            pltpu.VMEM(antenna_coords.T.shape, F32),
            pltpu.VMEM(baseline_antennas.T.shape, jnp.int32),
            pltpu.VMEM(filter_taps.shape, BF16),
            pltpu.VMEM((local_src, times), BF16),
            pltpu.VMEM((ROWS, local_src), BF16),
            pltpu.VMEM((local_src, ROWS), BF16),
            pltpu.VMEM((ROWS, 2 * times), BF16),
            pltpu.VMEM((n_chan - own, 2 * group, local_src), BF16),
            pltpu.VMEM((n_chan - own, 2 * group, local_src), BF16),
            pltpu.VMEM((own, 2 * group, local_src) if own else (ROWS, 128), BF16),
            pltpu.VMEM((own, 2 * group, local_src) if own else (ROWS, 128), BF16),
            pltpu.VMEM((2, 4, group, local_src) if own else (8, 128), F32),
            pltpu.VMEM((n_chan, local_src, times), BF16),
            pltpu.VMEM((visible.shape[1], times), F32),
            pltpu.VMEM((GROUPS, 2 * group, ROWS), BF16),
            pltpu.VMEM((count, ROWS), F32),
            pltpu.VMEM((chans, TAIL + times, times), BF16),
            pltpu.VMEM((8, TAIL + times), F32),
            pltpu.VMEM((chans, 2, count, TAIL), BF16),
            pltpu.VMEM((2, far, chans, 2 * group, times), F32),
            pltpu.VMEM((GROUPS, chans, 2 * group, times), F32),
            pltpu.VMEM((GROUPS, chips, chans, 2 * group, times), BF16),
            pltpu.VMEM((GROUPS, chips, chans, 2 * group, times), BF16),
            pltpu.VMEM((GROUPS, far, chans, 2, group, times), BF16),
            pltpu.VMEM((GROUPS, chips, chans, 2, group, times), BF16),
            dma((8,)),
            dma((GROUPS, chips, chans)), dma((GROUPS, chips, chans)),
            dma((GROUPS, far, chans, PARTS)), dma((GROUPS, chips, chans, PARTS)),
            dma((GROUPS, chans, PARTS)), dma((GROUPS, chans, PARTS)),
        ],
        compiler_params=pltpu.CompilerParams(
            collective_id=0, has_side_effects=True, vmem_limit_bytes=64000000
        ),
    )(
        sky_east.reshape(rows), sky_north.reshape(rows), sky_flux.reshape(rows),
        visible, antenna_coords.T, baseline_antennas.T, filter_taps, sky_scint,
    )
    return pl.pallas_call(
        leave,
        out_shape=(shape, shape),
        in_specs=[vmem, vmem],
        out_specs=(hbm, hbm),
        scratch_shapes=[dma((2, chans, 2))],
        compiler_params=pltpu.CompilerParams(vmem_limit_bytes=1 << 20),
    )(vis, out)


def solution(mesh):
    return jax.shard_map(
        functools.partial(shards, mesh.shape["freq"], mesh.shape["lst"]),
        mesh=mesh,
        in_specs=(
            P(("trial", "freq")),
            P(("trial", "freq")),
            P(("trial", "freq")),
            P(("trial", "freq"), "lst"),
            P(("trial", "lst"), None),
            P(),
            P(),
            P("freq", None),
        ),
        out_specs=(
            P(("trial", "freq"), None, None, "lst"),
            P(("trial", "freq"), None, None, "lst"),
        ),
        check_vma=False,
    )
```

```python
import functools
import math

import jax
import jax.numpy as jnp
import numpy as np
from jax import lax
from jax.experimental import pallas as pl
from jax.experimental.pallas import tpu as pltpu
from jax.sharding import PartitionSpec as P

SRC_BLOCK = 128
TAIL = 256
BLOCK_T = 8

C_LIGHT = 299792458.0
NU_START = 150000000.0
NU_STEP = 97656.25
OMEGA_STEP = 4.37526e-05
BEAM_SIGMA = 0.35
CENTRE_START = -0.045
LOG2E = math.log2(math.e)
ROUNDER = 1.5 * 2.0**23
ROWS = 16
GROUPS = 4
PARTS = 2
TILE = 256
FIRST_TILE = 1024
AMP_TILE = 32
AMP_STEP = 1024
MESH = pl.DeviceIdType.MESH
F32 = jnp.float32
BF16 = jnp.bfloat16


def fit_even(fun, reach, degree):
    nodes = np.cos((np.arange(400) + 0.5) * np.pi / 400)
    z = 0.5 * reach * reach * (nodes + 1.0)
    cheb = np.polynomial.chebyshev.Chebyshev.fit(z, fun(np.sqrt(z)), degree, domain=[0.0, reach * reach])
    return [float(c) for c in cheb.convert(kind=np.polynomial.Polynomial).coef]


def cos_turn(x):
    return np.cos(2.0 * np.pi * x)


def sin_turn(x):
    return np.sin(2.0 * np.pi * x) / x


COS_FULL = fit_even(cos_turn, 0.5, 5)
SIN_FULL = fit_even(sin_turn, 0.5, 4)
STEP_REACH = 0.12
COS_STEP = fit_even(cos_turn, STEP_REACH, 3)
SIN_STEP = fit_even(sin_turn, STEP_REACH, 2)


def horner(coefs, z):
    total = coefs[-1] * z + coefs[-2]
    for c in coefs[-3::-1]:
        total = total * z + c
    return total


def cos_minus_sin(turns):
    r = turns - ((turns + ROUNDER) - ROUNDER)
    z = r * r
    return horner(COS_FULL, z), horner([-c for c in SIN_FULL], z) * r


def sincos_turns(turns):
    r = turns - ((turns + ROUNDER) - ROUNDER)
    z = r * r
    return horner(COS_FULL, z), horner(SIN_FULL, z) * r


def sincos_step(r):
    z = r * r
    return horner(COS_STEP, z), horner(SIN_STEP, z) * r


def pieces(x):
    high = x.astype(BF16).astype(F32)
    middle = (x - high).astype(BF16).astype(F32)
    low = (x - high - middle).astype(BF16).astype(F32)
    return high, middle, low


def rowdot(a, b):
    return lax.dot_general(a, b, (((0,), (0,)), ((), ())), preferred_element_type=F32)


def kernel(
    dims,
    east_hbm, north_hbm, flux_hbm, visible_hbm, coords_hbm, pairs_hbm, taps_hbm, scint_hbm,
    vis, out,
    east_ref, north_ref, flux_ref, visible_ref, coords_ref, pairs_ref, taps_ref,
    scint, phase_rows, beam_cols, beam_right, far_even, far_odd, own_even, own_odd, state, amps, mask_rows, coefs, lines, toep, tap_rows, tail, fringe,
    far_totals, own_totals, pair_out, pair_in, far_out, far_in,
    in_sems, pair_send, pair_recv, far_send, far_recv, halo_send, halo_recv,
):
    n_freq, n_lst, chans = dims
    local_src, times = scint.shape
    count = pairs_ref.shape[1]
    group = count // GROUPS
    part = group // PARTS
    chips = n_freq // 2
    per_chip = 2 * chans
    n_chan = chips * per_chip
    total_src = local_src * n_freq
    blocks = local_src // SRC_BLOCK
    me = lax.axis_index("freq")
    lst = lax.axis_index("lst")
    chip, core = me // 2, me % 2
    partner = chip * 2 + (1 - core)

    loads = [
        pltpu.make_async_copy(src, dst, in_sems.at[i])
        for i, (src, dst) in enumerate((
            (east_hbm, east_ref), (north_hbm, north_ref), (flux_hbm, flux_ref), (coords_hbm, coords_ref),
            (pairs_hbm, pairs_ref), (visible_hbm, visible_ref), (scint_hbm, scint), (taps_hbm, taps_ref),
        ))
    ]
    for load in loads:
        load.start()

    barrier = pltpu.get_barrier_semaphore()
    pl.semaphore_signal(barrier, inc=1, device_id={"freq": partner}, device_id_type=MESH)
    for d in range(1, chips):
        pl.semaphore_signal(
            barrier, inc=1, device_id={"freq": ((chip + d) % chips) * 2 + core}, device_id_type=MESH
        )

    @pl.when(lst > 0)
    def _():
        pl.semaphore_signal(barrier, inc=1, device_id={"lst": lst - 1}, device_id_type=MESH)

    def send(src, dst, ssem, rsem, to):
        return pltpu.make_async_remote_copy(
            src_ref=src, dst_ref=dst, send_sem=ssem, recv_sem=rsem, device_id=to, device_id_type=MESH
        )

    rising = chip * 2 >= chips
    way = jnp.where(rising, 1, -1)
    way_f = way.astype(F32)
    first = jnp.where(rising, 0, n_chan - 1).astype(F32)
    nu_first = NU_START + NU_STEP * first
    own_place = jnp.where(rising, chip, chips - 1 - chip)
    own_half = jnp.where(rising, core, 1 - core)
    nus = [NU_START + NU_STEP * (me * chans + c).astype(F32) for c in range(chans)]

    def place_of(d):
        return (own_place + d) % chips

    def chip_at(d):
        place = place_of(d)
        return jnp.where(rising, place, chips - 1 - place)

    def channel_at(q):
        return jnp.where(rising, q, chans - 1 - q)

    samples = (lst * times + lax.broadcasted_iota(jnp.int32, (1, times), 1)).astype(F32)
    centre = CENTRE_START + OMEGA_STEP * samples
    row_id = lax.broadcasted_iota(jnp.int32, (ROWS, times), 0)
    delta = NU_STEP / NU_START
    broad = 0.5 * LOG2E / (BEAM_SIGMA * BEAM_SIGMA)
    ratio = nu_first * (1.0 / NU_START)
    half = broad * ratio * ratio
    slope = broad * delta * way_f * (2.0 * ratio + delta * way_f)
    bend = 2.0 * broad * delta * delta / slope
    for at, scale, offset in ((0, half, 3), (1, slope, 9)):
        table = jnp.where((row_id >= offset) & (row_id < offset + 3), 1.0, 0.0)
        for base, rows in ((0, pieces(centre * (2.0 * scale))), (6, pieces(centre * centre * (-scale)))):
            for i, row in enumerate(rows):
                table = jnp.where(row_id == base + i, row, table)
        beam_right[:, at * times : (at + 1) * times] = table.astype(BF16)

    for load in loads[:6]:
        load.wait()
    l_all = east_ref[...].astype(F32)
    m_all = north_ref[...].astype(F32)
    radius = l_all * l_all + m_all * m_all
    level = jnp.log(flux_ref[...].astype(F32) * (1.0 / math.sqrt(total_src))) * LOG2E - radius * half
    level_rows = pieces(level)
    slope_rows = pieces(radius * (-slope))
    src_row = lax.broadcasted_iota(jnp.int32, (ROWS, SRC_BLOCK), 0)
    for k in range(blocks):
        at = slice(k, k + 1)
        rows = slice(k * SRC_BLOCK, (k + 1) * SRC_BLOCK)
        l = l_all[at]
        phase_rows[:, rows] = jnp.where(src_row < 3, l, jnp.where(src_row < 6, m_all[at], 0.0)).astype(BF16)
        table = jnp.where(src_row < 3, l, jnp.where(src_row < 9, 1.0, 0.0))
        for base, values in ((3, level_rows), (9, slope_rows)):
            for i, value in enumerate(values):
                table = jnp.where(src_row == base + i, value[at], table)
        beam_cols[rows, :] = table.T.astype(BF16)

    antennas = coords_ref.shape[1]
    ids = lax.broadcasted_iota(jnp.int32, (antennas, count), 0)
    select = ((pairs_ref[0:1, :] == ids).astype(F32) - (pairs_ref[1:2, :] == ids).astype(F32)).astype(BF16)
    place = jnp.concatenate([*pieces(coords_ref[...]), jnp.zeros((2, antennas), F32)], axis=0)
    picked = jnp.dot(place.astype(BF16), select, preferred_element_type=F32)
    both = (picked[4:6, :] + picked[2:4, :]) + picked[0:2, :]
    pair_row = lax.broadcasted_iota(jnp.int32, (ROWS, count), 0)

    def coef_rows(scale):
        table = jnp.where(pair_row == 6, both[0:1, :], 0.0)
        for base in range(2):
            for i, piece in enumerate(pieces(both[base : base + 1, :] * scale)):
                table = jnp.where(pair_row == 3 * base + i, piece, table)
        return table.T

    main = coef_rows(nu_first * (1.0 / C_LIGHT))
    step = coef_rows(way_f * (NU_STEP / C_LIGHT)).astype(BF16)
    lines[...] = main
    main = main.astype(BF16)
    for g in range(GROUPS):
        coefs[g, 0:group, :] = main[g * group : (g + 1) * group]
        coefs[g, group : 2 * group, :] = step[g * group : (g + 1) * group]

    t_blocks = visible_ref.shape[0]
    spread = (
        lax.broadcasted_iota(jnp.int32, (t_blocks, times), 1) // BLOCK_T
        == lax.broadcasted_iota(jnp.int32, (t_blocks, times), 0)
    ).astype(BF16)
    mask_rows[...] = rowdot(visible_ref[...].astype(F32).astype(BF16), spread)

    loads[6].wait()

    def amplitudes(start, end):
        for i in range(local_src // AMP_STEP):
            for k in range(AMP_STEP // AMP_TILE):
                rows = slice(i * AMP_STEP + k * AMP_TILE, i * AMP_STEP + (k + 1) * AMP_TILE)
                power = jnp.dot(beam_cols[rows, :], beam_right[...], preferred_element_type=F32)
                block = i * (AMP_STEP // SRC_BLOCK) + k // (SRC_BLOCK // AMP_TILE)
                mask = mask_rows[pl.ds(me * blocks + block, 1), :]
                log_value, log_gain = power[:, :times], power[:, times:]
                log_change = log_gain * bend
                if start > 0:
                    log_value = log_value + log_gain * (start + (0.5 * start * (start - 1)) * bend)
                    log_gain = log_gain + log_change * start
                value = jnp.exp2(log_value) * (scint[rows, :].astype(F32) * mask)
                gain = jnp.exp2(log_gain)
                change = jnp.exp2(log_change)
                for p in range(start, end):
                    amps[p, rows, :] = value.astype(BF16)
                    if p < end - 1:
                        value = value * gain
                    if p < end - 2:
                        gain = gain * change

    split = chips == 2
    middle = n_chan // 2 if split else n_chan
    planes = ((far_even, own_even), (far_odd, own_odd))

    def keep_planes(g, later, p, cols, co, si):
        planes[g % 2][later][p, 0:group, cols] = co.astype(BF16)
        planes[g % 2][later][p, group : 2 * group, cols] = si.astype(BF16)

    def turn_on(g, later, p, cols, co, si, cd, sd, number):
        twice = cd + cd
        older = None
        for i in range(number):
            keep_planes(g, later, p + i, cols, co, si)
            if i == number - 1:
                break
            if older is None:
                older, (co, si) = (co, si), (co * cd + si * sd, si * cd - co * sd)
            else:
                older, (co, si) = (co, si), (twice * co - older[0], twice * si - older[1])
        return co, si

    def trig_far(g, cols):
        turns = jnp.dot(coefs[g], phase_rows[:, cols], preferred_element_type=F32)
        co, si = cos_minus_sin(turns[:group])
        cd, sd = sincos_step(turns[group:])
        co, si = turn_on(g, 0, 0, cols, co, si, cd, sd, middle)
        if split:
            for i, value in enumerate((co, si, cd, sd)):
                state[g % 2, i, :, cols] = value

    def trig_own(g, cols):
        co, si, cd, sd = [state[g % 2, i, :, cols] for i in range(4)]
        turn_on(g, 1, 0, cols, co * cd + si * sd, si * cd - co * sd, cd, sd, n_chan - middle)

    def trig_first():
        for i in range(local_src // FIRST_TILE):
            trig_far(0, slice(i * FIRST_TILE, (i + 1) * FIRST_TILE))

    def partial_sum(g, d, half, q):
        if split:
            p = half * chans + q
            return jnp.dot(planes[g % 2][d == 0][p], amps[(d == 0) * middle + p], preferred_element_type=F32)
        p = place_of(d) * per_chip + half * chans + q
        return jnp.dot(planes[g % 2][0][p], amps[p], preferred_element_type=F32)

    def pair_copy(g, d, q):
        return send(
            pair_out.at[g, d, q], pair_in.at[g, d, q], pair_send.at[g, d, q], pair_recv.at[g, d, q], {"freq": partner}
        )

    def far_copy(g, d, c, h):
        rows = pl.ds(h * part, part)
        return send(
            far_out.at[g, d - 1, c, :, rows, :], far_in.at[g, chip, c, :, rows, :],
            far_send.at[g, d - 1, c, h], far_recv.at[g, chip, c, h], {"freq": chip_at(d) * 2 + core},
        )

    def far_arrival(g, d, c, h):
        src = (chip + d) % chips
        block = far_in.at[g, src, c, :, pl.ds(h * part, part), :]
        return send(block, block, far_send.at[g, d - 1, c, h], far_recv.at[g, src, c, h], {"freq": src * 2 + core})

    def group_rows(g):
        return pl.ds(g * group, group)

    def part_rows(g, h):
        at = g * group + h * part
        return pl.ds(at if isinstance(at, int) else pl.multiple_of(at, part), part)

    def halo_copy(g, c, h):
        rows = part_rows(g, h)
        return send(
            vis.at[c, :, rows, :], tail.at[c, :, rows, :], halo_send.at[g, c, h], halo_recv.at[g, c, h],
            {"lst": (lst + 1) % n_lst},
        )


    @pl.when(lst == 0)
    def _():
        tail[...] = jnp.zeros_like(tail)

    def kept_totals(g, d):
        return own_totals.at[g] if d == 0 else far_totals.at[g % 2, d - 1]

    def multiply(g, d, kept):
        for q in range(chans):
            if kept:
                kept_totals(g, d)[q] = partial_sum(g, d, own_half, q)
            else:
                pair_out[g, d, q] = partial_sum(g, d, 1 - own_half, q).astype(BF16)
                pair_copy(g, d, q).start()

    def forward(g):
        for d in range(1, chips):
            for q in range(chans):
                c = channel_at(q)
                pair_copy(g, d, q).wait_recv()
                for h in range(PARTS):
                    for r in range(2):
                        rows = slice(r * group + h * part, r * group + (h + 1) * part)
                        added = far_totals[g % 2, d - 1, q, rows, :] + pair_in[g, d, q, rows, :].astype(F32)
                        far_out[g, d - 1, c, r, h * part : (h + 1) * part, :] = added.astype(BF16)
                    far_copy(g, d, c, h).start()

    def spread_taps():
        loads[7].wait()
        tap_rows[...] = jnp.zeros_like(tap_rows)
        tap_rows[0:chans, 0 : TAIL + 1] = taps_ref[...].astype(F32)
        for c in range(chans):
            wide = jnp.broadcast_to(tap_rows[c : c + 1, :], (TAIL + times, TAIL + times))
            skewed = pltpu.roll(wide, 0, 1, stride=1, stride_axis=0)
            toep[c] = skewed[:, TAIL:].astype(BF16)

    def turn_fringe(g):
        rows = group_rows(g)
        for q in range(chans):
            scale = (NU_START + NU_STEP * (me * chans + channel_at(q)).astype(F32)) * (OMEGA_STEP / C_LIGHT)
            fringe[q, 0, rows, :], fringe[q, 1, rows, :] = sincos_turns((lines[rows, 6:7] * scale) * samples)

    def finish(g):
        for q in range(chans):
            c = channel_at(q)
            pair_copy(g, 0, q).wait_recv()
            for h in range(PARTS):
                rows = part_rows(g, h)
                for d in range(1, chips):
                    far_arrival(g, d, c, h).wait_recv()
                real, imag = [
                    sum(
                        (far_in[g, (chip + d) % chips, c, r, h * part : (h + 1) * part, :].astype(F32) for d in range(1, chips)),
                        start=own_totals[g, q, at, :] + pair_in[g, 0, q, at, :].astype(F32),
                    )
                    for r, at in enumerate(
                        slice(r * group + h * part, r * group + (h + 1) * part) for r in range(2)
                    )
                ]
                co, si = fringe[q, 0, rows, :], fringe[q, 1, rows, :]
                vis[c, 0, rows, :] = (co * real + si * imag).astype(BF16)
                vis[c, 1, rows, :] = (co * imag - si * real).astype(BF16)

                @pl.when(lst < n_lst - 1)
                def _():
                    halo_copy(g, c, h).start()


    def smooth_own(g):
        rows = group_rows(g)
        for q in range(chans):
            c = channel_at(q)
            block = vis[c, :, rows, :].reshape(2 * group, times)
            own_totals[g, q] = jnp.dot(block, toep[c, TAIL:, :], preferred_element_type=F32)

    def smooth_tail(g, q, first, last):
        c = channel_at(q)
        for h in range(first, last):

            @pl.when(lst > 0)
            def _():
                halo_copy(g, c, h).wait_recv()

        size = (last - first) * part
        rows = pl.ds(g * group + first * part, size)
        block = tail[c, :, rows, :].reshape(2 * size, TAIL)
        total = jnp.dot(block, toep[c, :TAIL, :], preferred_element_type=F32)
        for r in range(2):
            own = own_totals[g, q, r * group + first * part : r * group + last * part, :]
            out[c, r, rows, :] = (total[r * size : (r + 1) * size] + own).astype(BF16)

    def smooth(g):
        for q in range(chans):
            smooth_tail(g, q, 0, PARTS)

    tiles = local_src // TILE

    def multiply_beside(g, stages, trig, new):
        for i in range(max(tiles, len(stages))):
            if i < len(stages):
                multiply(g, *stages[i])
            if i < tiles and trig is not None and new < GROUPS:
                trig(new, slice(i * TILE, (i + 1) * TILE))

    far_stages = [(d, kept) for d in range(1, chips) for kept in (False, True)]
    own_stages = [(0, False), (0, True)]
    own_trig = trig_own if split else None
    amplitudes(0, middle)
    trig_first()
    pl.semaphore_wait(barrier, chips + (lst < n_lst - 1).astype(jnp.int32))
    multiply_beside(0, far_stages, None, 0)
    if split:
        amplitudes(middle, n_chan)
    turn_fringe(0)
    forward(0)
    for i in range(tiles):
        trig_far(1, slice(i * TILE, (i + 1) * TILE))
    def conclude(g):
        if g > 1:
            smooth(g - 2)
        finish(g)
        if g < GROUPS - 1:
            turn_fringe(g + 1)
        if g == 0:
            spread_taps()
        smooth_own(g)

    for g in range(GROUPS):
        if g < GROUPS - 1:
            multiply_beside(g + 1, far_stages, own_trig, g)
        else:
            multiply_beside(g, [], own_trig, g)
        if g > 0:
            conclude(g - 1)
        if split:
            multiply_beside(g, own_stages, trig_far, g + 2)
        else:
            multiply_beside(g, own_stages, None, 0)
            multiply_beside(g, [], trig_far, g + 2)
        if g < GROUPS - 1:
            forward(g + 1)
    conclude(GROUPS - 1)
    smooth(GROUPS - 2)
    for q in range(chans):
        for h in range(PARTS):
            smooth_tail(GROUPS - 1, q, h, h + 1)

    @pl.loop(0, GROUPS)
    def _(g):
        for d in range(chips):
            for q in range(chans):
                pair_copy(g, d, q).wait_send()
        for c in range(chans):
            for h in range(PARTS):
                for d in range(1, chips):
                    far_copy(g, d, c, h).wait_send()

                @pl.when(lst < n_lst - 1)
                def _():
                    halo_copy(g, c, h).wait_send()


def leave(vis, out, vis_hbm, out_hbm, sems):
    copies = [
        pltpu.make_async_copy(src.at[c, r], dst.at[c, r], sems.at[i, c, r])
        for i, (src, dst) in enumerate(((vis, vis_hbm), (out, out_hbm)))
        for c in range(vis.shape[0])
        for r in range(2)
    ]
    for copy in copies:
        copy.start()
    for copy in copies:
        copy.wait()


def shards(n_freq, n_lst, sky_east, sky_north, sky_flux, sky_scint, visible, antenna_coords, baseline_antennas, filter_taps):
    chans = filter_taps.shape[0]
    local_src, times = sky_scint.shape
    count = baseline_antennas.shape[0]
    group = count // GROUPS
    chips = n_freq // 2
    n_chan = chans * n_freq
    held = pltpu.VMEM((chans, 2, count, times), BF16)
    shape = jax.ShapeDtypeStruct((chans, 2, count, times), BF16)
    vmem = pl.BlockSpec(memory_space=pltpu.VMEM)
    hbm = pl.BlockSpec(memory_space=pl.ANY)
    dma = pltpu.SemaphoreType.DMA
    far = max(chips - 1, 1)
    own = n_chan // 2 if chips == 2 else 0
    rows = (local_src // 128, 128)
    vis, out = pl.pallas_call(
        functools.partial(kernel, (n_freq, n_lst, chans)),
        out_shape=(held, held),
        in_specs=[hbm] * 8,
        out_specs=(vmem, vmem),
        scratch_shapes=[
            pltpu.VMEM(rows, BF16), pltpu.VMEM(rows, BF16), pltpu.VMEM(rows, BF16),
            pltpu.VMEM(visible.shape, jnp.int32),
            pltpu.VMEM(antenna_coords.T.shape, F32),
            pltpu.VMEM(baseline_antennas.T.shape, jnp.int32),
            pltpu.VMEM(filter_taps.shape, BF16),
            pltpu.VMEM((local_src, times), BF16),
            pltpu.VMEM((ROWS, local_src), BF16),
            pltpu.VMEM((local_src, ROWS), BF16),
            pltpu.VMEM((ROWS, 2 * times), BF16),
            pltpu.VMEM((n_chan - own, 2 * group, local_src), BF16),
            pltpu.VMEM((n_chan - own, 2 * group, local_src), BF16),
            pltpu.VMEM((own, 2 * group, local_src) if own else (ROWS, 128), BF16),
            pltpu.VMEM((own, 2 * group, local_src) if own else (ROWS, 128), BF16),
            pltpu.VMEM((2, 4, group, local_src) if own else (8, 128), F32),
            pltpu.VMEM((n_chan, local_src, times), BF16),
            pltpu.VMEM((visible.shape[1], times), F32),
            pltpu.VMEM((GROUPS, 2 * group, ROWS), BF16),
            pltpu.VMEM((count, ROWS), F32),
            pltpu.VMEM((chans, TAIL + times, times), BF16),
            pltpu.VMEM((8, TAIL + times), F32),
            pltpu.VMEM((chans, 2, count, TAIL), BF16),
            pltpu.VMEM((chans, 2, count, times), F32),
            pltpu.VMEM((2, far, chans, 2 * group, times), F32),
            pltpu.VMEM((GROUPS, chans, 2 * group, times), F32),
            pltpu.VMEM((GROUPS, chips, chans, 2 * group, times), BF16),
            pltpu.VMEM((GROUPS, chips, chans, 2 * group, times), BF16),
            pltpu.VMEM((GROUPS, far, chans, 2, group, times), BF16),
            pltpu.VMEM((GROUPS, chips, chans, 2, group, times), BF16),
            dma((8,)),
            dma((GROUPS, chips, chans)), dma((GROUPS, chips, chans)),
            dma((GROUPS, far, chans, PARTS)), dma((GROUPS, chips, chans, PARTS)),
            dma((GROUPS, chans, PARTS)), dma((GROUPS, chans, PARTS)),
        ],
        compiler_params=pltpu.CompilerParams(
            collective_id=0, has_side_effects=True, vmem_limit_bytes=64000000
        ),
    )(
        sky_east.reshape(rows), sky_north.reshape(rows), sky_flux.reshape(rows),
        visible, antenna_coords.T, baseline_antennas.T, filter_taps, sky_scint,
    )
    return pl.pallas_call(
        leave,
        out_shape=(shape, shape),
        in_specs=[vmem, vmem],
        out_specs=(hbm, hbm),
        scratch_shapes=[dma((2, chans, 2))],
        compiler_params=pltpu.CompilerParams(vmem_limit_bytes=1 << 20),
    )(vis, out)


def solution(mesh):
    return jax.shard_map(
        functools.partial(shards, mesh.shape["freq"], mesh.shape["lst"]),
        mesh=mesh,
        in_specs=(
            P(("trial", "freq")),
            P(("trial", "freq")),
            P(("trial", "freq")),
            P(("trial", "freq"), "lst"),
            P(("trial", "lst"), None),
            P(),
            P(),
            P("freq", None),
        ),
        out_specs=(
            P(("trial", "freq"), None, None, "lst"),
            P(("trial", "freq"), None, None, "lst"),
        ),
        check_vma=False,
    )
```

```python
import functools
import math

import jax
import jax.numpy as jnp
import numpy as np
from jax import lax
from jax.experimental import pallas as pl
from jax.experimental.pallas import tpu as pltpu
from jax.sharding import PartitionSpec as P

SRC_BLOCK = 128
TAIL = 256
BLOCK_T = 8

C_LIGHT = 299792458.0
NU_START = 150000000.0
NU_STEP = 97656.25
OMEGA_STEP = 4.37526e-05
BEAM_SIGMA = 0.35
CENTRE_START = -0.045
LOG2E = math.log2(math.e)
ROUNDER = 1.5 * 2.0**23
ROWS = 16
GROUPS = 4
PARTS = 1
TILE = 256
FIRST_TILE = 1024
AMP_TILE = 32
AMP_STEP = 1024
MESH = pl.DeviceIdType.MESH
F32 = jnp.float32
BF16 = jnp.bfloat16


def fit_even(fun, reach, degree):
    nodes = np.cos((np.arange(400) + 0.5) * np.pi / 400)
    z = 0.5 * reach * reach * (nodes + 1.0)
    cheb = np.polynomial.chebyshev.Chebyshev.fit(z, fun(np.sqrt(z)), degree, domain=[0.0, reach * reach])
    return [float(c) for c in cheb.convert(kind=np.polynomial.Polynomial).coef]


def cos_turn(x):
    return np.cos(2.0 * np.pi * x)


def sin_turn(x):
    return np.sin(2.0 * np.pi * x) / x


COS_FULL = fit_even(cos_turn, 0.5, 5)
SIN_FULL = fit_even(sin_turn, 0.5, 4)
STEP_REACH = 0.12
COS_STEP = fit_even(cos_turn, STEP_REACH, 3)
SIN_STEP = fit_even(sin_turn, STEP_REACH, 2)


def horner(coefs, z):
    total = coefs[-1] * z + coefs[-2]
    for c in coefs[-3::-1]:
        total = total * z + c
    return total


def cos_minus_sin(turns):
    r = turns - ((turns + ROUNDER) - ROUNDER)
    z = r * r
    return horner(COS_FULL, z), horner([-c for c in SIN_FULL], z) * r


def sincos_turns(turns):
    r = turns - ((turns + ROUNDER) - ROUNDER)
    z = r * r
    return horner(COS_FULL, z), horner(SIN_FULL, z) * r


def sincos_step(r):
    z = r * r
    return horner(COS_STEP, z), horner(SIN_STEP, z) * r


def pieces(x):
    high = x.astype(BF16).astype(F32)
    middle = (x - high).astype(BF16).astype(F32)
    low = (x - high - middle).astype(BF16).astype(F32)
    return high, middle, low


def rowdot(a, b):
    return lax.dot_general(a, b, (((0,), (0,)), ((), ())), preferred_element_type=F32)


def kernel(
    dims,
    east_hbm, north_hbm, flux_hbm, visible_hbm, coords_hbm, pairs_hbm, taps_hbm, scint_hbm,
    vis, out,
    east_ref, north_ref, flux_ref, visible_ref, coords_ref, pairs_ref, taps_ref,
    scint, phase_rows, beam_cols, beam_right, far_even, far_odd, own_even, own_odd, state, amps, mask_rows, coefs, lines, toep, tap_rows, tail, fringe,
    far_totals, own_totals, pair_out, pair_in, far_out, far_in,
    in_sems, pair_send, pair_recv, far_send, far_recv, halo_send, halo_recv,
):
    n_freq, n_lst, chans = dims
    local_src, times = scint.shape
    count = pairs_ref.shape[1]
    group = count // GROUPS
    part = group // PARTS
    chips = n_freq // 2
    per_chip = 2 * chans
    n_chan = chips * per_chip
    total_src = local_src * n_freq
    blocks = local_src // SRC_BLOCK
    me = lax.axis_index("freq")
    lst = lax.axis_index("lst")
    chip, core = me // 2, me % 2
    partner = chip * 2 + (1 - core)

    loads = [
        pltpu.make_async_copy(src, dst, in_sems.at[i])
        for i, (src, dst) in enumerate((
            (east_hbm, east_ref), (north_hbm, north_ref), (flux_hbm, flux_ref), (coords_hbm, coords_ref),
            (pairs_hbm, pairs_ref), (visible_hbm, visible_ref), (scint_hbm, scint), (taps_hbm, taps_ref),
        ))
    ]
    for load in loads:
        load.start()

    barrier = pltpu.get_barrier_semaphore()
    pl.semaphore_signal(barrier, inc=1, device_id={"freq": partner}, device_id_type=MESH)
    for d in range(1, chips):
        pl.semaphore_signal(
            barrier, inc=1, device_id={"freq": ((chip + d) % chips) * 2 + core}, device_id_type=MESH
        )

    @pl.when(lst > 0)
    def _():
        pl.semaphore_signal(barrier, inc=1, device_id={"lst": lst - 1}, device_id_type=MESH)

    def send(src, dst, ssem, rsem, to):
        return pltpu.make_async_remote_copy(
            src_ref=src, dst_ref=dst, send_sem=ssem, recv_sem=rsem, device_id=to, device_id_type=MESH
        )

    rising = chip * 2 >= chips
    way = jnp.where(rising, 1, -1)
    way_f = way.astype(F32)
    first = jnp.where(rising, 0, n_chan - 1).astype(F32)
    nu_first = NU_START + NU_STEP * first
    own_place = jnp.where(rising, chip, chips - 1 - chip)
    own_half = jnp.where(rising, core, 1 - core)
    nus = [NU_START + NU_STEP * (me * chans + c).astype(F32) for c in range(chans)]

    def place_of(d):
        return (own_place + d) % chips

    def chip_at(d):
        place = place_of(d)
        return jnp.where(rising, place, chips - 1 - place)

    def channel_at(q):
        return jnp.where(rising, q, chans - 1 - q)

    samples = (lst * times + lax.broadcasted_iota(jnp.int32, (1, times), 1)).astype(F32)
    centre = CENTRE_START + OMEGA_STEP * samples
    row_id = lax.broadcasted_iota(jnp.int32, (ROWS, times), 0)
    delta = NU_STEP / NU_START
    broad = 0.5 * LOG2E / (BEAM_SIGMA * BEAM_SIGMA)
    ratio = nu_first * (1.0 / NU_START)
    half = broad * ratio * ratio
    slope = broad * delta * way_f * (2.0 * ratio + delta * way_f)
    bend = 2.0 * broad * delta * delta / slope
    for at, scale, offset in ((0, half, 3), (1, slope, 9)):
        table = jnp.where((row_id >= offset) & (row_id < offset + 3), 1.0, 0.0)
        for base, rows in ((0, pieces(centre * (2.0 * scale))), (6, pieces(centre * centre * (-scale)))):
            for i, row in enumerate(rows):
                table = jnp.where(row_id == base + i, row, table)
        beam_right[:, at * times : (at + 1) * times] = table.astype(BF16)

    for load in loads[:6]:
        load.wait()
    l_all = east_ref[...].astype(F32)
    m_all = north_ref[...].astype(F32)
    radius = l_all * l_all + m_all * m_all
    level = jnp.log(flux_ref[...].astype(F32) * (1.0 / math.sqrt(total_src))) * LOG2E - radius * half
    level_rows = pieces(level)
    slope_rows = pieces(radius * (-slope))
    src_row = lax.broadcasted_iota(jnp.int32, (ROWS, SRC_BLOCK), 0)
    for k in range(blocks):
        at = slice(k, k + 1)
        rows = slice(k * SRC_BLOCK, (k + 1) * SRC_BLOCK)
        l = l_all[at]
        phase_rows[:, rows] = jnp.where(src_row < 3, l, jnp.where(src_row < 6, m_all[at], 0.0)).astype(BF16)
        table = jnp.where(src_row < 3, l, jnp.where(src_row < 9, 1.0, 0.0))
        for base, values in ((3, level_rows), (9, slope_rows)):
            for i, value in enumerate(values):
                table = jnp.where(src_row == base + i, value[at], table)
        beam_cols[rows, :] = table.T.astype(BF16)

    antennas = coords_ref.shape[1]
    ids = lax.broadcasted_iota(jnp.int32, (antennas, count), 0)
    select = ((pairs_ref[0:1, :] == ids).astype(F32) - (pairs_ref[1:2, :] == ids).astype(F32)).astype(BF16)
    place = jnp.concatenate([*pieces(coords_ref[...]), jnp.zeros((2, antennas), F32)], axis=0)
    picked = jnp.dot(place.astype(BF16), select, preferred_element_type=F32)
    both = (picked[4:6, :] + picked[2:4, :]) + picked[0:2, :]
    pair_row = lax.broadcasted_iota(jnp.int32, (ROWS, count), 0)

    def coef_rows(scale):
        table = jnp.where(pair_row == 6, both[0:1, :], 0.0)
        for base in range(2):
            for i, piece in enumerate(pieces(both[base : base + 1, :] * scale)):
                table = jnp.where(pair_row == 3 * base + i, piece, table)
        return table.T

    main = coef_rows(nu_first * (1.0 / C_LIGHT))
    step = coef_rows(way_f * (NU_STEP / C_LIGHT)).astype(BF16)
    lines[...] = main
    main = main.astype(BF16)
    for g in range(GROUPS):
        coefs[g, 0:group, :] = main[g * group : (g + 1) * group]
        coefs[g, group : 2 * group, :] = step[g * group : (g + 1) * group]

    t_blocks = visible_ref.shape[0]
    spread = (
        lax.broadcasted_iota(jnp.int32, (t_blocks, times), 1) // BLOCK_T
        == lax.broadcasted_iota(jnp.int32, (t_blocks, times), 0)
    ).astype(BF16)
    mask_rows[...] = rowdot(visible_ref[...].astype(F32).astype(BF16), spread)

    loads[6].wait()

    def amplitudes(start, end):
        for i in range(local_src // AMP_STEP):
            for k in range(AMP_STEP // AMP_TILE):
                rows = slice(i * AMP_STEP + k * AMP_TILE, i * AMP_STEP + (k + 1) * AMP_TILE)
                power = jnp.dot(beam_cols[rows, :], beam_right[...], preferred_element_type=F32)
                block = i * (AMP_STEP // SRC_BLOCK) + k // (SRC_BLOCK // AMP_TILE)
                mask = mask_rows[pl.ds(me * blocks + block, 1), :]
                log_value, log_gain = power[:, :times], power[:, times:]
                log_change = log_gain * bend
                if start > 0:
                    log_value = log_value + log_gain * (start + (0.5 * start * (start - 1)) * bend)
                    log_gain = log_gain + log_change * start
                value = jnp.exp2(log_value) * (scint[rows, :].astype(F32) * mask)
                gain = jnp.exp2(log_gain)
                change = jnp.exp2(log_change)
                for p in range(start, end):
                    amps[p, rows, :] = value.astype(BF16)
                    if p < end - 1:
                        value = value * gain
                    if p < end - 2:
                        gain = gain * change

    split = chips == 2
    middle = n_chan // 2 if split else n_chan
    planes = ((far_even, own_even), (far_odd, own_odd))

    def keep_planes(g, later, p, cols, co, si):
        planes[g % 2][later][p, 0:group, cols] = co.astype(BF16)
        planes[g % 2][later][p, group : 2 * group, cols] = si.astype(BF16)

    def turn_on(g, later, p, cols, co, si, cd, sd, number):
        twice = cd + cd
        older = None
        for i in range(number):
            keep_planes(g, later, p + i, cols, co, si)
            if i == number - 1:
                break
            if older is None:
                older, (co, si) = (co, si), (co * cd + si * sd, si * cd - co * sd)
            else:
                older, (co, si) = (co, si), (twice * co - older[0], twice * si - older[1])
        return co, si

    def trig_far(g, cols):
        turns = jnp.dot(coefs[g], phase_rows[:, cols], preferred_element_type=F32)
        co, si = cos_minus_sin(turns[:group])
        cd, sd = sincos_step(turns[group:])
        co, si = turn_on(g, 0, 0, cols, co, si, cd, sd, middle)
        if split:
            for i, value in enumerate((co, si, cd, sd)):
                state[g % 2, i, :, cols] = value

    def trig_own(g, cols):
        co, si, cd, sd = [state[g % 2, i, :, cols] for i in range(4)]
        turn_on(g, 1, 0, cols, co * cd + si * sd, si * cd - co * sd, cd, sd, n_chan - middle)

    def trig_first():
        for i in range(local_src // FIRST_TILE):
            trig_far(0, slice(i * FIRST_TILE, (i + 1) * FIRST_TILE))

    def partial_sum(g, d, half, q):
        if split:
            p = half * chans + q
            return jnp.dot(planes[g % 2][d == 0][p], amps[(d == 0) * middle + p], preferred_element_type=F32)
        p = place_of(d) * per_chip + half * chans + q
        return jnp.dot(planes[g % 2][0][p], amps[p], preferred_element_type=F32)

    def pair_copy(g, d, q):
        return send(
            pair_out.at[g, d, q], pair_in.at[g, d, q], pair_send.at[g, d, q], pair_recv.at[g, d, q], {"freq": partner}
        )

    def far_copy(g, d, c, h):
        rows = pl.ds(h * part, part)
        return send(
            far_out.at[g, d - 1, c, :, rows, :], far_in.at[g, chip, c, :, rows, :],
            far_send.at[g, d - 1, c, h], far_recv.at[g, chip, c, h], {"freq": chip_at(d) * 2 + core},
        )

    def far_arrival(g, d, c, h):
        src = (chip + d) % chips
        block = far_in.at[g, src, c, :, pl.ds(h * part, part), :]
        return send(block, block, far_send.at[g, d - 1, c, h], far_recv.at[g, src, c, h], {"freq": src * 2 + core})

    def group_rows(g):
        return pl.ds(g * group, group)

    def part_rows(g, h):
        at = g * group + h * part
        return pl.ds(at if isinstance(at, int) else pl.multiple_of(at, part), part)

    def halo_copy(g, c, h):
        rows = part_rows(g, h)
        return send(
            vis.at[c, :, rows, :], tail.at[c, :, rows, :], halo_send.at[g, c, h], halo_recv.at[g, c, h],
            {"lst": (lst + 1) % n_lst},
        )


    @pl.when(lst == 0)
    def _():
        tail[...] = jnp.zeros_like(tail)

    def kept_totals(g, d):
        return own_totals.at[g] if d == 0 else far_totals.at[g % 2, d - 1]

    def multiply(g, d, kept):
        for q in range(chans):
            if kept:
                kept_totals(g, d)[q] = partial_sum(g, d, own_half, q)
            else:
                pair_out[g, d, q] = partial_sum(g, d, 1 - own_half, q).astype(BF16)
                pair_copy(g, d, q).start()

    def forward(g):
        for d in range(1, chips):
            for q in range(chans):
                c = channel_at(q)
                pair_copy(g, d, q).wait_recv()
                for h in range(PARTS):
                    for r in range(2):
                        rows = slice(r * group + h * part, r * group + (h + 1) * part)
                        added = far_totals[g % 2, d - 1, q, rows, :] + pair_in[g, d, q, rows, :].astype(F32)
                        far_out[g, d - 1, c, r, h * part : (h + 1) * part, :] = added.astype(BF16)
                    far_copy(g, d, c, h).start()

    def spread_taps():
        loads[7].wait()
        tap_rows[...] = jnp.zeros_like(tap_rows)
        tap_rows[0:chans, 0 : TAIL + 1] = taps_ref[...].astype(F32)
        for c in range(chans):
            wide = jnp.broadcast_to(tap_rows[c : c + 1, :], (TAIL + times, TAIL + times))
            skewed = pltpu.roll(wide, 0, 1, stride=1, stride_axis=0)
            toep[c] = skewed[:, TAIL:].astype(BF16)

    def turn_fringe(g):
        rows = group_rows(g)
        for q in range(chans):
            scale = (NU_START + NU_STEP * (me * chans + channel_at(q)).astype(F32)) * (OMEGA_STEP / C_LIGHT)
            fringe[q, 0, rows, :], fringe[q, 1, rows, :] = sincos_turns((lines[rows, 6:7] * scale) * samples)

    def finish(g):
        for q in range(chans):
            c = channel_at(q)
            pair_copy(g, 0, q).wait_recv()
            for h in range(PARTS):
                rows = part_rows(g, h)
                for d in range(1, chips):
                    far_arrival(g, d, c, h).wait_recv()
                real, imag = [
                    sum(
                        (far_in[g, (chip + d) % chips, c, r, h * part : (h + 1) * part, :].astype(F32) for d in range(1, chips)),
                        start=own_totals[g, q, at, :] + pair_in[g, 0, q, at, :].astype(F32),
                    )
                    for r, at in enumerate(
                        slice(r * group + h * part, r * group + (h + 1) * part) for r in range(2)
                    )
                ]
                co, si = fringe[q, 0, rows, :], fringe[q, 1, rows, :]
                vis[c, 0, rows, :] = (co * real + si * imag).astype(BF16)
                vis[c, 1, rows, :] = (co * imag - si * real).astype(BF16)

                @pl.when(lst < n_lst - 1)
                def _():
                    halo_copy(g, c, h).start()


    def smooth_own(g):
        rows = group_rows(g)
        for q in range(chans):
            c = channel_at(q)
            block = vis[c, :, rows, :].reshape(2 * group, times)
            own_totals[g, q] = jnp.dot(block, toep[c, TAIL:, :], preferred_element_type=F32)

    def smooth_tail(g, q, first, last):
        c = channel_at(q)
        for h in range(first, last):

            @pl.when(lst > 0)
            def _():
                halo_copy(g, c, h).wait_recv()

        size = (last - first) * part
        rows = pl.ds(g * group + first * part, size)
        block = tail[c, :, rows, :].reshape(2 * size, TAIL)
        total = jnp.dot(block, toep[c, :TAIL, :], preferred_element_type=F32)
        for r in range(2):
            own = own_totals[g, q, r * group + first * part : r * group + last * part, :]
            out[c, r, rows, :] = (total[r * size : (r + 1) * size] + own).astype(BF16)

    def smooth(g):
        for q in range(chans):
            smooth_tail(g, q, 0, PARTS)

    tiles = local_src // TILE

    def multiply_beside(g, stages, trig, new):
        for i in range(max(tiles, len(stages))):
            if i < len(stages):
                multiply(g, *stages[i])
            if i < tiles and trig is not None and new < GROUPS:
                trig(new, slice(i * TILE, (i + 1) * TILE))

    far_stages = [(d, kept) for d in range(1, chips) for kept in (False, True)]
    own_stages = [(0, False), (0, True)]
    own_trig = trig_own if split else None
    amplitudes(0, middle)
    trig_first()
    pl.semaphore_wait(barrier, chips + (lst < n_lst - 1).astype(jnp.int32))
    multiply_beside(0, far_stages, None, 0)
    if split:
        amplitudes(middle, n_chan)
    turn_fringe(0)
    forward(0)
    for i in range(tiles):
        trig_far(1, slice(i * TILE, (i + 1) * TILE))
    def conclude(g):
        if g > 1:
            smooth(g - 2)
        finish(g)
        if g < GROUPS - 1:
            turn_fringe(g + 1)
        if g == 0:
            spread_taps()
        smooth_own(g)

    for g in range(GROUPS):
        if g < GROUPS - 1:
            multiply_beside(g + 1, far_stages, own_trig, g)
        else:
            multiply_beside(g, [], own_trig, g)
        if g > 0:
            conclude(g - 1)
        if split:
            multiply_beside(g, own_stages, trig_far, g + 2)
        else:
            multiply_beside(g, own_stages, None, 0)
            multiply_beside(g, [], trig_far, g + 2)
        if g < GROUPS - 1:
            forward(g + 1)
    conclude(GROUPS - 1)
    smooth(GROUPS - 2)
    for q in range(chans):
        for h in range(PARTS):
            smooth_tail(GROUPS - 1, q, h, h + 1)

    @pl.loop(0, GROUPS)
    def _(g):
        for d in range(chips):
            for q in range(chans):
                pair_copy(g, d, q).wait_send()
        for c in range(chans):
            for h in range(PARTS):
                for d in range(1, chips):
                    far_copy(g, d, c, h).wait_send()

                @pl.when(lst < n_lst - 1)
                def _():
                    halo_copy(g, c, h).wait_send()


def leave(vis, out, vis_hbm, out_hbm, sems):
    copies = [
        pltpu.make_async_copy(src.at[c, r], dst.at[c, r], sems.at[i, c, r])
        for i, (src, dst) in enumerate(((vis, vis_hbm), (out, out_hbm)))
        for c in range(vis.shape[0])
        for r in range(2)
    ]
    for copy in copies:
        copy.start()
    for copy in copies:
        copy.wait()


def shards(n_freq, n_lst, sky_east, sky_north, sky_flux, sky_scint, visible, antenna_coords, baseline_antennas, filter_taps):
    chans = filter_taps.shape[0]
    local_src, times = sky_scint.shape
    count = baseline_antennas.shape[0]
    group = count // GROUPS
    chips = n_freq // 2
    n_chan = chans * n_freq
    held = pltpu.VMEM((chans, 2, count, times), BF16)
    shape = jax.ShapeDtypeStruct((chans, 2, count, times), BF16)
    vmem = pl.BlockSpec(memory_space=pltpu.VMEM)
    hbm = pl.BlockSpec(memory_space=pl.ANY)
    dma = pltpu.SemaphoreType.DMA
    far = max(chips - 1, 1)
    own = n_chan // 2 if chips == 2 else 0
    rows = (local_src // 128, 128)
    vis, out = pl.pallas_call(
        functools.partial(kernel, (n_freq, n_lst, chans)),
        out_shape=(held, held),
        in_specs=[hbm] * 8,
        out_specs=(vmem, vmem),
        scratch_shapes=[
            pltpu.VMEM(rows, BF16), pltpu.VMEM(rows, BF16), pltpu.VMEM(rows, BF16),
            pltpu.VMEM(visible.shape, jnp.int32),
            pltpu.VMEM(antenna_coords.T.shape, F32),
            pltpu.VMEM(baseline_antennas.T.shape, jnp.int32),
            pltpu.VMEM(filter_taps.shape, BF16),
            pltpu.VMEM((local_src, times), BF16),
            pltpu.VMEM((ROWS, local_src), BF16),
            pltpu.VMEM((local_src, ROWS), BF16),
            pltpu.VMEM((ROWS, 2 * times), BF16),
            pltpu.VMEM((n_chan - own, 2 * group, local_src), BF16),
            pltpu.VMEM((n_chan - own, 2 * group, local_src), BF16),
            pltpu.VMEM((own, 2 * group, local_src) if own else (ROWS, 128), BF16),
            pltpu.VMEM((own, 2 * group, local_src) if own else (ROWS, 128), BF16),
            pltpu.VMEM((2, 4, group, local_src) if own else (8, 128), F32),
            pltpu.VMEM((n_chan, local_src, times), BF16),
            pltpu.VMEM((visible.shape[1], times), F32),
            pltpu.VMEM((GROUPS, 2 * group, ROWS), BF16),
            pltpu.VMEM((count, ROWS), F32),
            pltpu.VMEM((chans, TAIL + times, times), BF16),
            pltpu.VMEM((8, TAIL + times), F32),
            pltpu.VMEM((chans, 2, count, TAIL), BF16),
            pltpu.VMEM((chans, 2, count, times), F32),
            pltpu.VMEM((2, far, chans, 2 * group, times), F32),
            pltpu.VMEM((GROUPS, chans, 2 * group, times), F32),
            pltpu.VMEM((GROUPS, chips, chans, 2 * group, times), BF16),
            pltpu.VMEM((GROUPS, chips, chans, 2 * group, times), BF16),
            pltpu.VMEM((GROUPS, far, chans, 2, group, times), BF16),
            pltpu.VMEM((GROUPS, chips, chans, 2, group, times), BF16),
            dma((8,)),
            dma((GROUPS, chips, chans)), dma((GROUPS, chips, chans)),
            dma((GROUPS, far, chans, PARTS)), dma((GROUPS, chips, chans, PARTS)),
            dma((GROUPS, chans, PARTS)), dma((GROUPS, chans, PARTS)),
        ],
        compiler_params=pltpu.CompilerParams(
            collective_id=0, has_side_effects=True, vmem_limit_bytes=64000000
        ),
    )(
        sky_east.reshape(rows), sky_north.reshape(rows), sky_flux.reshape(rows),
        visible, antenna_coords.T, baseline_antennas.T, filter_taps, sky_scint,
    )
    return pl.pallas_call(
        leave,
        out_shape=(shape, shape),
        in_specs=[vmem, vmem],
        out_specs=(hbm, hbm),
        scratch_shapes=[dma((2, chans, 2))],
        compiler_params=pltpu.CompilerParams(vmem_limit_bytes=1 << 20),
    )(vis, out)


def solution(mesh):
    return jax.shard_map(
        functools.partial(shards, mesh.shape["freq"], mesh.shape["lst"]),
        mesh=mesh,
        in_specs=(
            P(("trial", "freq")),
            P(("trial", "freq")),
            P(("trial", "freq")),
            P(("trial", "freq"), "lst"),
            P(("trial", "lst"), None),
            P(),
            P(),
            P("freq", None),
        ),
        out_specs=(
            P(("trial", "freq"), None, None, "lst"),
            P(("trial", "freq"), None, None, "lst"),
        ),
        check_vma=False,
    )
```
